32 devices in a mesh: gx: 8 (over y, x, core), gy: 4 (over z).
Axes of the slice: x: 2, y: 2, z: 4, core: 2. Of those that a mesh axis runs over, the one named last changes fastest.
Arguments:
- displacement: float32 [3, 16, 8, 128], P(None, 'gx', 'gy'), may hold values from -0.3 to 0.3
- velocity: float32 [3, 16, 8, 128], P(None, 'gx', 'gy'), may hold values from -30 to 30
- forces: float32 [3, 16, 8, 128], P(None, 'gx', 'gy'), may hold values from -30 to 30
- heights: int32 [16, 8, 128], P('gx', 'gy'), may hold values from 0 to 127, as said below
- counts: int32 [16, 8], P('gx', 'gy'), may hold values from 64 to 128
- neighbours: int32 [8, 16, 8, 128], P(None, 'gx', 'gy'), may hold values from 0 to 1151, as said below
- plan: int32 [8, 4, 4, 1], P('gx', 'gy'), may hold values from 0 to 3; in each aligned block of 4 rows (0 to 3, 4 to 7, ..., all dimensions but the last counted through in order) at most 2 rows name the same one
Outputs:
- arrived: float32 [8, 4, 4, 2, 7, 128], P('gx', 'gy')
The draws below stay inside these ranges and needn't reach their ends.
Inputs may be any that keep to these rules, and one draw needn't show every extreme that they name: `heights`: each cell column's 128 entries name every layer from 0 to 127 once. `neighbours`: entry c * 128 + s names slot s of the column at offset (c // 3 - 1, c % 3 - 1) in x and y; a slot never names itself. `plan`: among one device's 2 * 2 cell columns at most 2 name the same new owner.
All inputs are finite; a program needn't handle non-finite values.
Results may differ from the reference program's by a relative error of at most 0.0003.
Values sent between devices are 32-bit elements; how exact they have to be, the bound alone decides.
No kernel may reach another device: no remote copies, remote signals or barrier semaphores. Data moves between devices by JAX's collectives and lax.ppermute only.
A program may use at most 64 MiB of HBM per device.

```python
import math
import jax
import jax.numpy as jnp
import numpy as np
from jax import lax

CX = 2
CY = 2
S = 128
K = 8
STEPS = 1
NXC = 16
NYC = 8
CAP = 2
N_GX = 8
N_GY = 4


def layout_tables(key):
    base_key = jax.random.fold_in(key, 11)
    key_order, key_cell, key_slot, key_shuffle = jax.random.split(base_key, 4)
    ramp = jnp.arange(S, dtype=jnp.int32)
    scores = jax.random.randint(key_order, (NXC, NYC, S), 0, 1 << 20) * S + ramp
    layers = jnp.argsort(scores, axis=-1).astype(jnp.int32)
    slot_of = jnp.argsort(layers, axis=-1).astype(jnp.int32)
    entries = []
    for shift_x, shift_y in ((-1, 0), (1, 0), (0, -1), (0, 1)):
        position = (shift_x + 1) * 3 + (shift_y + 1)
        moved = jnp.roll(jnp.roll(slot_of, -shift_x, axis=0), -shift_y, axis=1)
        entries.append(position * S + jnp.take_along_axis(moved, layers, axis=2))
    for change in (-1, 1):
        target = (layers + change + S) % S
        entries.append(4 * S + jnp.take_along_axis(slot_of, target, axis=2))
    extra_cell = jax.random.randint(key_cell, (2, NXC, NYC, S), 0, 8)
    extra_cell = extra_cell + (extra_cell >= 4).astype(jnp.int32)
    extra_slot = jax.random.randint(key_slot, (2, NXC, NYC, S), 0, S)
    entries.append(extra_cell[0] * S + extra_slot[0])
    entries.append(extra_cell[1] * S + extra_slot[1])
    lists = jnp.stack(entries, axis=0).astype(jnp.int32)
    shuffle_scores = jax.random.randint(key_shuffle, (8, NXC, NYC, S), 0, 1 << 20) * 8 + jnp.arange(8, dtype=jnp.int32)[:, None, None, None]
    order = jnp.argsort(shuffle_scores, axis=0)
    lists = jnp.take_along_axis(lists, order, axis=0).astype(jnp.int32)
    return (layers, lists)


def draw_heights(key, part):
    layers, lists = layout_tables(key)
    return layers


def draw_neighbours(key, part):
    layers, lists = layout_tables(key)
    return lists


def place_ends(drawn, own_key, low, top_value):
    spot = [jax.random.randint(jax.random.fold_in(own_key, axis), (), 0, length) for axis, length in enumerate(drawn.shape)]
    widest = drawn.shape.index(max(drawn.shape))
    beside = spot[:widest] + [(spot[widest] + 1) % drawn.shape[widest]] + spot[widest + 1:]
    return drawn.at[tuple(spot)].set(low).at[tuple(beside)].set(top_value)


def shard_levels(own_key, dims, shards, least, high):
    gain, own = 1.0, jax.random.fold_in(own_key, 6)
    for axis_at, blocks in shards:
        steps = jnp.exp(jax.random.uniform(jax.random.fold_in(own, axis_at), (blocks,), jnp.float32, least / len(shards), high / len(shards)))
        gain = gain * jnp.repeat(steps, dims[axis_at] // blocks).reshape([-1 if axis == axis_at else 1 for axis in range(len(dims))])
    return gain


def deal_out(stream_key, own, number, rows, amount, top, reach, lean):
    sequence = jax.random.permutation(stream_key, amount)
    crowded, ordinary = load_shares(amount, rows * top, reach, lean, True), load_shares(amount, rows * top, reach, lean, False)
    places = jnp.arange(amount)

    def named(lengths, offset_by):
        used = int((lengths > 0).sum())
        fixed = max(1, used // 4)
        passed = fixed + (places - fixed + offset_by * (used - fixed)) % max(1, amount - fixed)
        return jnp.zeros((amount,), jnp.int32).at[sequence[jnp.where(places < fixed, places, passed)]].set(jnp.asarray(lengths, jnp.int32))

    lengths = jnp.where(number % 4 == 0, named(crowded, number // 4), named(ordinary, number - number // 4 - 1))
    mixed = jax.random.permutation(jax.random.fold_in(own, 3), amount)
    giver, taker = mixed[0:amount // 2 * 2:2], mixed[1:amount // 2 * 2:2]
    slack = jnp.minimum(lengths[giver] - 1, reach - lengths[taker]) // 2
    slack = jnp.where((giver == sequence[0]) | (taker == sequence[0]) | (lengths[taker] == 0), 0, jnp.maximum(slack, 0))
    passed = jax.random.randint(jax.random.fold_in(own, 4), (amount // 2,), 0, 1 << 20) % (slack + 1)
    lengths = lengths.at[giver].add(-passed).at[taker].add(passed)
    members = jnp.searchsorted(jnp.cumsum(lengths), jnp.arange(rows * top), side="right").astype(jnp.int32)
    grid = members.reshape(top, rows).T
    grid = grid[jax.random.permutation(jax.random.fold_in(own, 1), rows)]
    offset_by = jax.random.randint(jax.random.fold_in(own, 2), (rows, 1), 0, top)
    return jnp.take_along_axis(grid, (jnp.arange(top)[None, :] + offset_by) % top, axis=1)


def load_shares(count, total, limit, lean, full):
    loads = [(1 << 20) // math.isqrt(grade ** lean) + 1 for grade in range(1, count + 1)]
    largest = limit if full else min(limit, max(-(-total // count), total * loads[0] // sum(loads)))
    least = 1 if total - largest >= count - 1 else 0
    given, spare = [largest] + [least] * (count - 1), total - largest - least * (count - 1)
    while spare > 0:
        candidates = [i for i in range(1, count) if given[i] < largest] or [i for i in range(1, count) if given[i] < limit]
        pool, remaining = sum([loads[i] for i in candidates]), spare
        for i in candidates:
            extra = min(limit - given[i], max(1, remaining * loads[i] // pool), spare)
            given[i] = given[i] + extra
            spare = spare - extra
    return np.array(given)


def bell_draw(rng, dims, width, bound, cuts=(), kind=jnp.bfloat16):
    values = width * jax.random.normal(rng, dims, jnp.float32)
    if cuts:
        values = values * shard_levels(rng, dims, cuts, -0.22, 0.18)
    return jnp.clip(values, -bound, bound).astype(kind)


def setup_inputs(seed: int = 0) -> dict:
    keys = jax.random.split(jax.random.key(seed), 8)
    displacement = bell_draw(keys[0], (3, NXC, NYC, S), 0.1, 0.3, ((1, 8), (2, 4)), jnp.float32)
    velocity = bell_draw(keys[1], (3, NXC, NYC, S), 5.0, 30.0, ((1, 8), (2, 4)), jnp.float32)
    forces = bell_draw(keys[2], (3, NXC, NYC, S), 5.0, 30.0, ((1, 8), (2, 4)), jnp.float32)
    heights = draw_heights(jax.random.fold_in(keys[7], 71), 0)
    counts = place_ends(jax.random.randint(keys[4], (NXC, NYC), S // 2, S + 1), jax.random.fold_in(keys[4], 1), S // 2, S).astype(jnp.int32)
    neighbours = draw_neighbours(jax.random.fold_in(keys[7], 71), 0)
    plan_keys = jax.random.split(jax.random.fold_in(keys[6], 1), N_GX * N_GY * (CX * CY) // (CX * CY))
    plan_turns = jax.random.permutation(jax.random.fold_in(keys[6], 3), N_GX * N_GY * (CX * CY) // (CX * CY))
    plan = jax.vmap(lambda own, number: deal_out(jax.random.fold_in(keys[6], 2), own, number, CX * CY, N_GY, 1, CAP, 2))(plan_keys, plan_turns).reshape((N_GX, N_GY, CX * CY, 1))
    return dict(displacement=displacement, velocity=velocity, forces=forces, heights=heights, counts=counts, neighbours=neighbours, plan=plan)


repulse_a = 1830.8
attract_b = 471.18
decay_one = 2.4799
decay_two = 1.7322
beta_t = 1.1e-06
expo_n = 0.78734
coeff_c2 = 100390.0 ** 2
coeff_d2 = 16.217 ** 2
coeff_h = -0.59825
spacing = 2.4
time_step = 0.001
half_step = 0.0005
force_scale = 9648.53 / 28.0855

def cutoff(radius):
    smooth = 0.5 - 0.5 * jnp.sin(0.5 * jnp.pi * (radius - 2.85) / 0.15)
    return jnp.where(radius < 2.7, 1.0, jnp.where(radius > 3.0, 0.0, smooth))

def cell_energy(center, nearby):
    offsets = nearby[:3] - center[:3][:, :, :, None, :]
    radius = jnp.sqrt(jnp.maximum(lax.optimization_barrier(jnp.sum(offsets * offsets, axis=0)), 1.0))
    weight = cutoff(radius) * nearby[3]
    direction = offsets / radius
    cosine = direction[0][:, :, :, None, :] * direction[0][:, :, None, :, :]
    cosine = cosine + direction[1][:, :, :, None, :] * direction[1][:, :, None, :, :]
    cosine = cosine + direction[2][:, :, :, None, :] * direction[2][:, :, None, :, :]
    spread = (coeff_h - cosine) ** 2
    angular = 1.0 + coeff_c2 * spread / (coeff_d2 * (coeff_d2 + spread))
    others = 1.0 - jnp.eye(nearby.shape[3], dtype=cosine.dtype)[:, :, None]
    bond_sum = jnp.maximum(lax.optimization_barrier(jnp.sum(angular * weight[:, :, None, :, :] * others, axis=3)), 1.0)
    bond_order = (1.0 + jnp.exp(expo_n * jnp.log(beta_t * bond_sum))) ** (-0.5 / expo_n)
    pair_terms = weight * (repulse_a * jnp.exp(-decay_one * radius) - attract_b * jnp.exp(-decay_two * radius) * bond_order)
    return 0.5 * center[3] * lax.optimization_barrier(jnp.sum(pair_terms, axis=2))

def flat_index(neighbours):
    width_x, width_y = (neighbours.shape[1], neighbours.shape[2])
    return jnp.transpose(neighbours, (1, 2, 0, 3)).reshape(width_x, width_y, -1)

def gather_nearby(points, gather_index):
    width_x, width_y = (gather_index.shape[0], gather_index.shape[1])
    slots = points.shape[3]
    pieces = [points[:, 1 + shift_x:1 + shift_x + width_x, 1 + shift_y:1 + shift_y + width_y] for shift_x in (-1, 0, 1) for shift_y in (-1, 0, 1)]
    joined = jnp.concatenate(pieces, axis=3)
    wide_index = jnp.broadcast_to(gather_index[None], (4,) + gather_index.shape)
    picked = jnp.take_along_axis(joined, wide_index, axis=3)
    return picked.reshape(4, width_x, width_y, gather_index.shape[2] // slots, slots)

def tersoff_total(coords, occupied, gather_index):
    points = jnp.concatenate([coords, occupied], axis=0)
    center = points[:, 1:-1, 1:-1]
    return jnp.sum(cell_energy(center, gather_nearby(points, gather_index)))

def global_forces(state, neighbours):
    padded = jnp.pad(state, ((0, 0), (2, 2), (2, 2), (0, 0)))
    wide = jnp.pad(neighbours, ((0, 0), (1, 1), (1, 1), (0, 0)))
    zero = jnp.zeros((), jnp.int32)

    def one_block(start):
        window = lax.dynamic_slice(padded, (zero, start, zero, zero), (4, CX + 4, NYC + 4, S))
        near_lists = lax.dynamic_slice(wide, (zero, start, zero, zero), (K, CX + 2, NYC + 2, S))
        grads = jax.grad(tersoff_total)(window[:3], window[3:], flat_index(near_lists))
        return -grads[:, 2:-2, 2:-2]
    starts = jnp.arange(N_GX, dtype=jnp.int32) * CX
    blocks = lax.map(one_block, starts)
    return jnp.transpose(blocks, (1, 0, 2, 3, 4)).reshape(3, NXC, NYC, S)

def pack_columns(rows, plan_rows, groups, capacity):
    target = plan_rows[:, 0]
    chosen = (target[:, None] == jnp.arange(groups, dtype=jnp.int32)[None, :]).astype(jnp.int32)
    earlier = jnp.cumsum(chosen, axis=0) - chosen
    place = target * capacity + lax.optimization_barrier(jnp.sum(chosen * earlier, axis=1))
    dispatch = (jnp.arange(groups * capacity, dtype=jnp.int32)[:, None] == place[None, :]).astype(rows.dtype)
    packed = jnp.einsum('rc,acs->ras', dispatch, rows, precision=lax.Precision.HIGHEST)
    return packed.reshape(groups, capacity, rows.shape[0], rows.shape[2])

def reference(displacement, velocity, forces, heights, counts, neighbours, plan):
    along_x = (jnp.arange(NXC, dtype=jnp.int32).astype(jnp.float32) + 0.5) * spacing
    along_y = (jnp.arange(NYC, dtype=jnp.int32).astype(jnp.float32) + 0.5) * spacing
    along_z = (heights.astype(jnp.float32) + 0.5) * spacing
    lattice = jnp.stack([jnp.broadcast_to(along_x[:, None, None], along_z.shape), jnp.broadcast_to(along_y[None, :, None], along_z.shape), along_z])
    occupied = (heights < counts[:, :, None]).astype(jnp.float32)
    offset, speed, force_now = (displacement, velocity, forces)
    for number in range(STEPS):
        speed = speed + half_step * (force_now * force_scale)
        offset = offset + time_step * speed
        state = jnp.concatenate([lattice + offset, occupied[None]], axis=0)
        force_now = global_forces(state, neighbours)
        speed = speed + half_step * (force_now * force_scale)
    rows = jnp.concatenate([offset, speed, occupied[None]], axis=0)
    blocks = rows.reshape(7, N_GX, CX, N_GY, CY, S).transpose(1, 3, 0, 2, 4, 5).reshape(N_GX, N_GY, 7, CX * CY, S)
    packed = jax.vmap(jax.vmap(lambda part_rows, part_plan: pack_columns(part_rows, part_plan, N_GY, CAP)))(blocks, plan)
    return jnp.swapaxes(packed, 1, 2)
```

```python
import functools

import jax
import jax.numpy as jnp
from jax import lax
from jax.experimental import pallas as pl
from jax.experimental.pallas import tpu as pltpu
from jax.sharding import PartitionSpec as P

repulse_a = 1830.8
attract_b = 471.18
decay_one = 2.4799
decay_two = 1.7322
beta_t = 1.1e-06
expo_n = 0.78734
coeff_c2 = 100390.0**2
coeff_d2 = 16.217**2
coeff_h = -0.59825
spacing = 2.4
time_step = 0.001
half_step = 0.0005
force_scale = 9648.53 / 28.0855
far_away = 1.0e6
half_pi = 1.5707963267948966
ROWS = 8

VMEM = pltpu.MemorySpace.VMEM
SMEM = pltpu.MemorySpace.SMEM


def line_partner(place, count, odd):
    other = ((place - 1) ^ 1) + 1 if odd else place ^ 1
    return other if 0 <= other < count else None


def exchange_pairs(counts, axis, odd):
    pairs = []
    for a in range(counts[0]):
        for b in range(counts[1]):
            here = [a, b]
            other = line_partner(here[axis], counts[axis], odd)
            if other is not None:
                here[axis] = other
            else:
                spare = line_partner(here[1 - axis], counts[1 - axis], False)
                if spare is None:
                    continue
                here[1 - axis] = spare
            pairs.append((a * counts[1] + b, here[0] * counts[1] + here[1]))
    return pairs


def round_partner(place, turn, count):
    ring = count - 1
    other = lax.rem(turn - place + 2 * ring, ring)
    alone = turn * ((ring + 1) // 2) % ring
    return jnp.where(place == ring, alone, jnp.where(place == alone, ring, other))


def round_pairs(counts, turn):
    ring = counts[1] - 1
    alone = turn * ((ring + 1) // 2) % ring
    pairs = []
    for a in range(counts[0]):
        for b in range(counts[1]):
            other = alone if b == ring else ring if b == alone else (turn - b) % ring
            pairs.append((a * counts[1] + b, a * counts[1] + other))
    return pairs


def prepare_kernel(disp, vel, force, heights, counts, lists, plan, rows, send_a, send_b, *, capacity):
    _, cells_x, cells_y, slots = disp.shape
    entries = lists.shape[0]
    at_x, at_y = lax.axis_index("gx"), lax.axis_index("gy")
    even_x = lax.rem(at_x, 2) == 0
    for x in range(cells_x):
        base_x = ((at_x * cells_x + x).astype(jnp.float32) + 0.5) * spacing
        for y in range(cells_y):
            base_y = ((at_y * cells_y + y).astype(jnp.float32) + 0.5) * spacing
            layer = heights[x, pl.ds(y, 1), :]
            occupied = (layer < counts[x, y]).astype(jnp.float32)
            lattice = (base_x, base_y, (layer.astype(jnp.float32) + 0.5) * spacing)
            column = (x * cells_y + y) * ROWS
            for q in range(3):
                pick = (q, x, pl.ds(y, 1), slice(None))
                speed = vel[pick] + half_step * (force[pick] * force_scale)
                offset = disp[pick] + time_step * speed
                rows[pl.ds(column + q, 1), :] = offset
                rows[pl.ds(column + 3 + q, 1), :] = speed
                point = lattice[q] + offset
                place = (q * cells_y + y) * cells_x + x
                send_a[pl.ds(place, 1), :] = point
                send_b[pl.ds(place, 1), :] = point
            rows[pl.ds(column + 6, 1), :] = occupied
            owner = plan[x * cells_y + y]
            earlier = 0
            for c in range(x * cells_y + y):
                earlier = earlier + (plan[c] == owner).astype(jnp.int32)
            rows[pl.ds(column + 7, 1), :] = jnp.full(
                (1, slots), (owner * capacity + earlier).astype(jnp.float32)
            )
            place = (3 * cells_y + y) * cells_x + x
            send_a[pl.ds(place, 1), :] = occupied
            send_b[pl.ds(place, 1), :] = occupied
    base = 4 * cells_y * cells_x
    for m in range(entries):
        low = lists[m, 0].astype(jnp.float32)
        high = lists[m, cells_x - 1].astype(jnp.float32)
        send_a[pl.ds(base + m * cells_y, cells_y), :] = jnp.where(even_x, high, low)
        send_b[pl.ds(base + m * cells_y, cells_y), :] = jnp.where(even_x, low, high)


def strip_kernel(rows, own, got_a, got_b, middle, send_c, send_d, *, count_x, cells_x, cells_y):
    at_x, at_y = lax.axis_index("gx"), lax.axis_index("gy")
    even_x, even_y = lax.rem(at_x, 2) == 0, lax.rem(at_y, 2) == 0
    has_left = (at_x > 0).astype(jnp.float32)
    has_right = (at_x < count_x - 1).astype(jnp.float32)
    wide = cells_x + 4
    for q in range(4):
        for y in range(cells_y):
            place = (q * cells_y + y) * cells_x
            take = lambda ref: ref[pl.ds(place, cells_x), :]
            left = jnp.where(even_x, take(got_b), take(got_a))[cells_x - 2 :]
            right = jnp.where(even_x, take(got_a), take(got_b))[:2]
            if q == 3:
                left, right = left * has_left, right * has_right
            strip = jnp.concatenate([left, take(own), right], axis=0)
            middle[q, y] = strip
        low, high = middle[q, 0], middle[q, cells_y - 1]
        send_c[pl.ds(q * wide, wide), :] = jnp.where(even_y, high, low)
        send_d[pl.ds(q * wide, wide), :] = jnp.where(even_y, low, high)
    for x in range(cells_x):
        low = rows[pl.ds(x * cells_y * ROWS + 7, 1), :]
        high = rows[pl.ds((x * cells_y + cells_y - 1) * ROWS + 7, 1), :]
        send_c[pl.ds(4 * wide + x, 1), :] = jnp.where(even_y, high, low)
        send_d[pl.ds(4 * wide + x, 1), :] = jnp.where(even_y, low, high)


def half_wave(radius):
    angle = half_pi * (jnp.clip(radius, 2.7, 3.0) - 2.85) / 0.15
    square = angle * angle
    sine, cosine = 0.0, 0.0
    for odd in (15, 13, 11, 9, 7, 5, 3, 1):
        factor_s = 1.0
        for n in range(2, odd + 1):
            factor_s /= n
        factor_c = factor_s * odd
        sign = -1.0 if odd % 4 == 3 else 1.0
        sine = sine * square + sign * factor_s
        cosine = cosine * square + sign * factor_c
    return sine * angle, cosine


def step_gate(value):
    return jnp.where(value > 1.0, 1.0, jnp.where(value == 1.0, 0.5, 0.0))


def column_gradients(center, occupied, nearby):
    entries = len(nearby)
    each = range(entries)
    inverse, gate_r, weight, slope, unit, repulse, attract = [], [], [], [], [], [], []
    for m in each:
        offset = [nearby[m][q] - center[q] for q in range(3)]
        square = offset[0] * offset[0] + offset[1] * offset[1] + offset[2] * offset[2]
        bounded = jnp.maximum(square, 1.0)
        radius = jnp.sqrt(bounded)
        inverse.append(1.0 / radius)
        gate_r.append(step_gate(square))
        sine, cosine = half_wave(radius)
        inside, outside = radius < 2.7, radius > 3.0
        weight.append(jnp.where(inside, 1.0, jnp.where(outside, 0.0, 0.5 - 0.5 * sine)))
        slope.append(jnp.where(inside | outside, 0.0, (-0.5 * half_pi / 0.15) * cosine))
        unit.append([offset[q] * inverse[m] for q in range(3)])
        repulse.append(repulse_a * jnp.exp(-decay_one * radius))
        attract.append(attract_b * jnp.exp(-decay_two * radius))
    zero = jnp.zeros_like(occupied)
    total = [zero for _ in each]
    angular, tilt = {}, {}
    for m in each:
        for k in range(m + 1, entries):
            cosine = sum(unit[m][q] * unit[k][q] for q in range(3))
            lean = coeff_h - cosine
            spread = lean * lean
            part = 1.0 / (coeff_d2 + spread)
            value = 1.0 + (coeff_c2 / coeff_d2) * (spread * part)
            angular[m, k] = value
            tilt[m, k] = (-2.0 * coeff_c2) * lean * (part * part)
            total[m] = total[m] + weight[k] * value
            total[k] = total[k] + weight[m] * value
    half = 0.5 * occupied
    pull, by_weight, by_radius = [], [], []
    for m in each:
        bond_sum = jnp.maximum(total[m], 1.0)
        power = jnp.exp(expo_n * jnp.log(beta_t * bond_sum))
        bond = jnp.exp((-0.5 / expo_n) * jnp.log(1.0 + power))
        loss = 0.5 * bond * power / ((1.0 + power) * bond_sum)
        pull.append(half * weight[m] * attract[m] * loss * step_gate(total[m]))
        by_weight.append(half * (repulse[m] - attract[m] * bond))
        by_radius.append(
            half * weight[m] * (decay_two * attract[m] * bond - decay_one * repulse[m])
        )
    by_unit = [[zero] * 3 for _ in each]
    for m in each:
        for k in range(m + 1, entries):
            by_weight[m] = by_weight[m] + pull[k] * angular[m, k]
            by_weight[k] = by_weight[k] + pull[m] * angular[m, k]
            turn = (pull[m] * weight[k] + pull[k] * weight[m]) * tilt[m, k]
            for q in range(3):
                by_unit[m][q] = by_unit[m][q] + turn * unit[k][q]
                by_unit[k][q] = by_unit[k][q] + turn * unit[m][q]
    grads = []
    for m in each:
        across = [by_unit[m][q] * inverse[m] for q in range(3)]
        along = sum(across[q] * unit[m][q] for q in range(3))
        reach = gate_r[m] * (by_radius[m] + by_weight[m] * slope[m] - along)
        grads.append([across[q] + unit[m][q] * reach for q in range(3)])
    return grads


def force_kernel(
    rows, middle, got_a, got_b, got_c, got_d, lists, plan, *refs, counts, cells_x, cells_y, capacity, turns
):
    outs = refs[: len(turns) + 1] if turns else refs[:1]
    table, index, parts, hot, left_side, main, ghost = refs[len(outs) :]
    entries, slots = lists.shape[0], lists.shape[3]
    shift = slots.bit_length() - 1
    at_x, at_y = lax.axis_index("gx"), lax.axis_index("gy")
    even_x, even_y = lax.rem(at_x, 2) == 0, lax.rem(at_y, 2) == 0
    wide, near = cells_x + 4, cells_x + 2
    centers = near * cells_y
    base = 4 * cells_x * cells_y
    for m in range(entries):
        here = pl.ds(base + m * cells_y, cells_y)
        left = jnp.where(even_x, got_b[here, :], got_a[here, :]).astype(jnp.int32)
        right = jnp.where(even_x, got_a[here, :], got_b[here, :]).astype(jnp.int32)
        for y in range(cells_y):
            index[m, pl.ds(y * near, 1), :] = left[y : y + 1]
            for x in range(cells_x):
                index[m, pl.ds(y * near + 1 + x, 1), :] = lists[m, x, pl.ds(y, 1), :]
            index[m, pl.ds(y * near + near - 1, 1), :] = right[y : y + 1]
    has_below, has_above = at_y > 0, at_y < counts[1] - 1
    strips = []
    for y in range(-1, cells_y + 1):
        if 0 <= y < cells_y:
            strip = [middle[q, y] for q in range(4)]
        else:
            swap, there = (even_y, has_below) if y < 0 else (jnp.logical_not(even_y), has_above)
            strip = [
                jnp.where(swap, got_d[pl.ds(q * wide, wide), :], got_c[pl.ds(q * wide, wide), :])
                for q in range(4)
            ]
            strip[3] = strip[3] * there.astype(jnp.float32)
        strip[2] = jnp.where(strip[3] > 0.0, strip[2], far_away)
        for move in range(3):
            for q in range(4):
                table[q, move, pl.ds((y + 1) * near, near), :] = strip[q][move : move + near]
    center = [table[q, 1, pl.ds(near, centers), :] for q in range(4)]
    occupied = center[3]
    entry_slot, entry_cell = [], []
    for m in range(entries):
        value = index[m]
        entry_slot.append(value & (slots - 1))
        entry_cell.append(value >> shift)
    nearby = [[None] * 3 for _ in range(entries)]
    for q in range(3):
        for c in range(9):
            source = table[q, c // 3, pl.ds((c % 3) * near, centers), :]
            for m in range(entries):
                picked = jnp.take_along_axis(
                    source, entry_slot[m], axis=1, mode="promise_in_bounds"
                )
                nearby[m][q] = (
                    picked if c == 0 else jnp.where(entry_cell[m] == c, picked, nearby[m][q])
                )
    grads = column_gradients(center[:3], occupied, nearby)
    own = [sum(grads[m][q] for m in range(entries)) for q in range(3)]
    for m in range(entries):
        index[m] = entry_slot[m]
        for q in range(3):
            high = grads[m][q].astype(jnp.bfloat16).astype(jnp.float32)
            parts[m, 3 + q] = high
            parts[m, q] = grads[m][q] - high
        parts[m, 6] = entry_cell[m].astype(jnp.float32)
        parts[m, 7] = jnp.zeros_like(occupied)
    for q in range(3):
        parts[entries, q] = jnp.zeros_like(occupied)
        parts[entries, 3 + q] = own[q]
    for q in (6, 7):
        parts[entries, q] = jnp.zeros_like(occupied)
    reached = {}
    ramp = lax.broadcasted_iota(jnp.int32, (slots, slots), 0)
    for y in range(cells_y):
        for x in range(-1, cells_x + 1):
            i = y * near + x + 1
            targets = [
                (dx, dy) for dx in (-1, 0, 1) if 0 <= x + dx < cells_x for dy in (-1, 0, 1)
            ]
            for m in range(entries):
                lanes = pl.ds(m * slots, slots)
                row = jnp.broadcast_to(index[m, pl.ds(i, 1), :], (slots, slots))
                hot[:, lanes] = jnp.where(ramp == row, 1.0, 0.0).astype(jnp.bfloat16)
                values = parts[m, :, i, :]
                cell = jnp.broadcast_to(parts[m, 6, pl.ds(i, 1), :], (ROWS, slots))
                masked = []
                for dx, dy in targets:
                    c = (dx + 1) * 3 + dy + 1
                    masked.append(jnp.where(cell == float(c), values, 0.0))
                left_side[pl.ds(0, ROWS * len(targets)), lanes] = jnp.concatenate(
                    masked, axis=0
                ).astype(jnp.bfloat16)
            sums = lax.dot_general(
                left_side[pl.ds(0, ROWS * len(targets)), :],
                hot[...],
                (((1,), (1,)), ((), ())),
                preferred_element_type=jnp.float32,
            )
            for n, (dx, dy) in enumerate(targets):
                key = (x + dx, y + dy)
                block = sums[n * ROWS : (n + 1) * ROWS]
                reached[key] = block if key not in reached else reached[key] + block
    line = lax.broadcasted_iota(jnp.int32, (ROWS, slots), 0)
    kick = half_step * force_scale
    chosen = (line >= 3) & (line < 6)
    main[...] = jnp.zeros_like(main)
    for x in range(cells_x):
        for y in range(-1, cells_y + 1):
            block = reached[x, y]
            block = block + pltpu.roll(block, 3, 0)
            if 0 <= y < cells_y:
                block = parts[entries, :, y * near + x + 1, :] - block
                column = rows[pl.ds((x * cells_y + y) * ROWS, ROWS), :]
                column = column + jnp.where(chosen, kick * block, 0.0)
                owner = plan[x * cells_y + y]
                earlier = 0
                for c in range(x * cells_y + y):
                    earlier = earlier + (plan[c] == owner).astype(jnp.int32)
                main[owner, pl.ds(earlier * 7, 7), :] = column[:7]
            else:
                ghost[0 if y < 0 else 1, x] = -kick * block
    places = [4 * wide + x for x in range(cells_x)]
    below = [jnp.where(even_y, got_d[pl.ds(p, 1), :], got_c[pl.ds(p, 1), :]) for p in places]
    above = [jnp.where(even_y, got_c[pl.ds(p, 1), :], got_d[pl.ds(p, 1), :]) for p in places]
    size = main.shape[1]

    def message(owner):
        pieces = [main[owner]]
        for side, named in enumerate((below, above)):
            for slot in range(capacity):
                wanted = (owner * capacity + slot).astype(jnp.float32)
                piece = 0.0
                for x in range(cells_x):
                    piece = piece + jnp.where(named[x] == wanted, ghost[side, x, pl.ds(3, 3), :], 0.0)
                pieces.append(piece)
        return pieces

    def write(ref, pieces):
        first = 0
        for piece in pieces:
            ref[pl.ds(first, piece.shape[0]), :] = piece
            first += piece.shape[0]

    if turns:
        for ref, turn in zip(outs[:-1], turns):
            write(ref, message(round_partner(at_y, turn, counts[1])))
        write(outs[-1], message(at_y))
    else:
        for owner in range(counts[1]):
            write(outs[0].at[owner], message(jnp.int32(owner)))


def gather_kernel(*refs, count, capacity, turns):
    at_y = lax.axis_index("gy")
    if turns:
        ins, out, held = refs[:-2], refs[-2], refs[-1]
        for ref, turn in zip(ins[:-1], turns):
            held[round_partner(at_y, turn, count)] = ref[...]
        held[at_y] = ins[-1][...]
    else:
        held, out = refs
    first = capacity * 7
    for source in range(count):
        for slot in range(capacity):
            block = held[source, pl.ds(slot * 7, 7), :]
            speed = block[3:6]
            if source + 1 < count:
                speed = speed + held[source + 1, pl.ds(first + slot * 3, 3), :]
            if source > 0:
                speed = speed + held[source - 1, pl.ds(first + (capacity + slot) * 3, 3), :]
            out[source, slot, pl.ds(0, 3), :] = block[:3]
            out[source, slot, pl.ds(3, 3), :] = speed
            out[source, slot, pl.ds(6, 1), :] = block[6:7]


def per_device(displacement, velocity, forces, heights, counts, neighbours, plan):
    cells_x, cells_y, slots = heights.shape
    entries = neighbours.shape[0]
    sizes = (lax.axis_size("gx"), lax.axis_size("gy"))
    columns = cells_x * cells_y
    capacity = max(2, (2 * columns + sizes[1] - 1) // sizes[1])
    owners = plan.reshape(columns)
    whole, scalar = pl.BlockSpec(memory_space=VMEM), pl.BlockSpec(memory_space=SMEM)
    shape = lambda *dims: jax.ShapeDtypeStruct(dims, jnp.float32)
    wide, near = cells_x + 4, cells_x + 2
    centers = near * cells_y

    def swap(value, pairs):
        return lax.ppermute(value, ("gx", "gy"), pairs)

    first_size = 4 * columns + entries * cells_y
    rows, send_a, send_b = pl.pallas_call(
        functools.partial(prepare_kernel, capacity=capacity),
        out_shape=(shape(columns * ROWS, slots), shape(first_size, slots), shape(first_size, slots)),
        in_specs=[whole, whole, whole, whole, scalar, whole, scalar],
        out_specs=(whole, whole, whole),
        name="prepare",
    )(displacement, velocity, forces, heights, counts, neighbours, owners)
    got_a = swap(send_a, exchange_pairs(sizes, 0, False))
    got_b = swap(send_b, exchange_pairs(sizes, 0, True))
    second_size = 4 * wide + cells_x
    middle, send_c, send_d = pl.pallas_call(
        functools.partial(strip_kernel, count_x=sizes[0], cells_x=cells_x, cells_y=cells_y),
        out_shape=(shape(4, cells_y, wide, slots), shape(second_size, slots), shape(second_size, slots)),
        in_specs=[whole] * 4,
        out_specs=(whole, whole, whole),
        name="strips",
    )(rows, send_a, got_a, got_b)
    got_c = swap(send_c, exchange_pairs(sizes, 1, False))
    got_d = swap(send_d, exchange_pairs(sizes, 1, True))
    turns = tuple(range(sizes[1] - 1)) if sizes[1] in (2, 4) else ()
    size = capacity * 13
    out_shape = (shape(size, slots),) * (len(turns) + 1) if turns else (shape(sizes[1], size, slots),)
    sent = pl.pallas_call(
        functools.partial(
            force_kernel, counts=sizes, cells_x=cells_x, cells_y=cells_y, capacity=capacity, turns=turns
        ),
        out_shape=out_shape,
        in_specs=[whole] * 7 + [scalar],
        out_specs=tuple(whole for _ in out_shape),
        scratch_shapes=[
            pltpu.VMEM((4, 3, near * (cells_y + 2), slots), jnp.float32),
            pltpu.VMEM((entries, centers, slots), jnp.int32),
            pltpu.VMEM((entries + 1, ROWS, centers, slots), jnp.float32),
            pltpu.VMEM((slots, entries * slots), jnp.bfloat16),
            pltpu.VMEM((9 * ROWS, entries * slots), jnp.bfloat16),
            pltpu.VMEM((sizes[1], capacity * 7, slots), jnp.float32),
            pltpu.VMEM((2, cells_x, ROWS, slots), jnp.float32),
        ],
        name="forces",
    )(rows, middle, got_a, got_b, got_c, got_d, neighbours, owners)
    if turns:
        arrived = [swap(value, round_pairs(sizes, turn)) for value, turn in zip(sent, turns)]
        arrived.append(sent[-1])
        scratch = [pltpu.VMEM((sizes[1], size, slots), jnp.float32)]
    else:
        arrived = [lax.all_to_all(sent[0], "gy", split_axis=0, concat_axis=0, tiled=True)]
        scratch = []
    result = pl.pallas_call(
        functools.partial(gather_kernel, count=sizes[1], capacity=capacity, turns=turns),
        out_shape=shape(sizes[1], capacity, 7, slots),
        in_specs=[whole] * len(arrived),
        out_specs=whole,
        scratch_shapes=scratch,
        name="collect",
    )(*arrived)
    return result[None, None]


def solution(mesh):
    in_specs = (
        P(None, "gx", "gy", None),
        P(None, "gx", "gy", None),
        P(None, "gx", "gy", None),
        P("gx", "gy", None),
        P("gx", "gy"),
        P(None, "gx", "gy", None),
        P("gx", "gy", None, None),
    )
    out_specs = P("gx", "gy", None, None, None, None)
    return jax.shard_map(
        per_device, mesh=mesh, in_specs=in_specs, out_specs=out_specs, check_vma=False
    )
```

```python
import functools

import jax
import jax.numpy as jnp
from jax import lax
from jax.experimental import pallas as pl
from jax.experimental.pallas import tpu as pltpu
from jax.sharding import PartitionSpec as P

repulse_a = 1830.8
attract_b = 471.18
decay_one = 2.4799
decay_two = 1.7322
beta_t = 1.1e-06
expo_n = 0.78734
coeff_c2 = 100390.0**2
coeff_d2 = 16.217**2
coeff_h = -0.59825
spacing = 2.4
time_step = 0.001
half_step = 0.0005
force_scale = 9648.53 / 28.0855
far_away = 1.0e6
half_pi = 1.5707963267948966
VMEM_BYTES = 8 * 2**20
ROWS = 8

VMEM = pltpu.MemorySpace.VMEM
HBM = pltpu.MemorySpace.HBM


def line_partner(place, count, odd):
    other = ((place - 1) ^ 1) + 1 if odd else place ^ 1
    return other if 0 <= other < count else None


def exchange_pairs(counts, axis, odd):
    pairs = []
    for a in range(counts[0]):
        for b in range(counts[1]):
            here = [a, b]
            other = line_partner(here[axis], counts[axis], odd)
            if other is not None:
                here[axis] = other
            else:
                spare = line_partner(here[1 - axis], counts[1 - axis], False)
                if spare is None:
                    continue
                here[1 - axis] = spare
            pairs.append((a * counts[1] + b, here[0] * counts[1] + here[1]))
    return pairs


def round_partner(place, turn, count):
    ring = count - 1
    other = lax.rem(turn - place + 2 * ring, ring)
    alone = turn * ((ring + 1) // 2) % ring
    return jnp.where(place == ring, alone, jnp.where(place == alone, ring, other))


def round_pairs(counts, turn):
    ring = counts[1] - 1
    alone = turn * ((ring + 1) // 2) % ring
    pairs = []
    for a in range(counts[0]):
        for b in range(counts[1]):
            other = alone if b == ring else ring if b == alone else (turn - b) % ring
            pairs.append((a * counts[1] + b, a * counts[1] + other))
    return pairs


def prepare_kernel(*refs, capacity):
    count = 7
    sources, (rows, send_a, send_b) = refs[:count], refs[count : count + 3]
    held, done = refs[count + 3 : -1], refs[-1]
    copies = [
        pltpu.make_async_copy(source, target, done.at[n])
        for n, (source, target) in enumerate(zip(sources, held))
    ]
    for copy in copies:
        copy.start()
    disp, vel, force, heights, counts, lists, plan = held
    _, cells_x, cells_y, slots = disp.shape
    entries = lists.shape[0]
    at_x, at_y = lax.axis_index("gx"), lax.axis_index("gy")
    even_x = lax.rem(at_x, 2) == 0
    for copy in copies:
        copy.wait()
    owners = [plan[:, c : c + 1] for c in range(cells_x * cells_y)]
    for x in range(cells_x):
        base_x = ((at_x * cells_x + x).astype(jnp.float32) + 0.5) * spacing
        for y in range(cells_y):
            base_y = ((at_y * cells_y + y).astype(jnp.float32) + 0.5) * spacing
            layer = heights[x, pl.ds(y, 1), :]
            occupied = (layer < counts[x : x + 1, y : y + 1]).astype(jnp.float32)
            lattice = (base_x, base_y, (layer.astype(jnp.float32) + 0.5) * spacing)
            column = (x * cells_y + y) * ROWS
            for q in range(3):
                pick = (q, x, pl.ds(y, 1), slice(None))
                speed = vel[pick] + half_step * (force[pick] * force_scale)
                offset = disp[pick] + time_step * speed
                rows[pl.ds(column + q, 1), :] = offset
                rows[pl.ds(column + 3 + q, 1), :] = speed
                point = lattice[q] + offset
                place = (q * cells_y + y) * cells_x + x
                send_a[pl.ds(place, 1), :] = point
                send_b[pl.ds(place, 1), :] = point
            rows[pl.ds(column + 6, 1), :] = occupied
            owner = owners[x * cells_y + y]
            earlier = sum((owners[c] == owner).astype(jnp.int32) for c in range(x * cells_y + y))
            rows[pl.ds(column + 7, 1), :] = jnp.broadcast_to(
                (owner * capacity + earlier).astype(jnp.float32), (1, slots)
            )
            place = (3 * cells_y + y) * cells_x + x
            send_a[pl.ds(place, 1), :] = occupied
            send_b[pl.ds(place, 1), :] = occupied
    base = 4 * cells_y * cells_x
    for m in range(entries):
        low = lists[m, 0].astype(jnp.float32)
        high = lists[m, cells_x - 1].astype(jnp.float32)
        send_a[pl.ds(base + m * cells_y, cells_y), :] = jnp.where(even_x, high, low)
        send_b[pl.ds(base + m * cells_y, cells_y), :] = jnp.where(even_x, low, high)


def strip_kernel(rows, own, got_a, got_b, middle, send_c, send_d, *, count_x, cells_x, cells_y):
    at_x, at_y = lax.axis_index("gx"), lax.axis_index("gy")
    even_x, even_y = lax.rem(at_x, 2) == 0, lax.rem(at_y, 2) == 0
    has_left = (at_x > 0).astype(jnp.float32)
    has_right = (at_x < count_x - 1).astype(jnp.float32)
    wide = cells_x + 4
    for q in range(4):
        for y in range(cells_y):
            place = (q * cells_y + y) * cells_x
            take = lambda ref: ref[pl.ds(place, cells_x), :]
            left = jnp.where(even_x, take(got_b), take(got_a))[cells_x - 2 :]
            right = jnp.where(even_x, take(got_a), take(got_b))[:2]
            if q == 3:
                left, right = left * has_left, right * has_right
            strip = jnp.concatenate([left, take(own), right], axis=0)
            middle[q, y] = strip
        low, high = middle[q, 0], middle[q, cells_y - 1]
        send_c[pl.ds(q * wide, wide), :] = jnp.where(even_y, high, low)
        send_d[pl.ds(q * wide, wide), :] = jnp.where(even_y, low, high)
    for x in range(cells_x):
        low = rows[pl.ds(x * cells_y * ROWS + 7, 1), :]
        high = rows[pl.ds((x * cells_y + cells_y - 1) * ROWS + 7, 1), :]
        send_c[pl.ds(4 * wide + x, 1), :] = jnp.where(even_y, high, low)
        send_d[pl.ds(4 * wide + x, 1), :] = jnp.where(even_y, low, high)


def half_wave(radius):
    angle = half_pi * (jnp.clip(radius, 2.7, 3.0) - 2.85) / 0.15
    square = angle * angle
    sine, cosine = 0.0, 0.0
    for odd in (15, 13, 11, 9, 7, 5, 3, 1):
        factor_s = 1.0
        for n in range(2, odd + 1):
            factor_s /= n
        factor_c = factor_s * odd
        sign = -1.0 if odd % 4 == 3 else 1.0
        sine = sine * square + sign * factor_s
        cosine = cosine * square + sign * factor_c
    return sine * angle, cosine


def step_gate(value):
    return jnp.where(value > 1.0, 1.0, jnp.where(value == 1.0, 0.5, 0.0))


def column_gradients(center, occupied, nearby):
    entries = len(nearby)
    each = range(entries)
    inverse, gate_r, weight, slope, unit, repulse, attract = [], [], [], [], [], [], []
    for m in each:
        offset = [nearby[m][q] - center[q] for q in range(3)]
        square = offset[0] * offset[0] + offset[1] * offset[1] + offset[2] * offset[2]
        bounded = jnp.maximum(square, 1.0)
        radius = jnp.sqrt(bounded)
        inverse.append(1.0 / radius)
        gate_r.append(step_gate(square))
        sine, cosine = half_wave(radius)
        inside, outside = radius < 2.7, radius > 3.0
        weight.append(jnp.where(inside, 1.0, jnp.where(outside, 0.0, 0.5 - 0.5 * sine)))
        slope.append(jnp.where(inside | outside, 0.0, (-0.5 * half_pi / 0.15) * cosine))
        unit.append([offset[q] * inverse[m] for q in range(3)])
        repulse.append(repulse_a * jnp.exp(-decay_one * radius))
        attract.append(attract_b * jnp.exp(-decay_two * radius))
    zero = jnp.zeros_like(occupied)
    total = [zero for _ in each]
    angular, tilt = {}, {}
    for m in each:
        for k in range(m + 1, entries):
            cosine = sum(unit[m][q] * unit[k][q] for q in range(3))
            lean = coeff_h - cosine
            spread = lean * lean
            part = 1.0 / (coeff_d2 + spread)
            value = 1.0 + (coeff_c2 / coeff_d2) * (spread * part)
            angular[m, k] = value
            tilt[m, k] = (-2.0 * coeff_c2) * lean * (part * part)
            total[m] = total[m] + weight[k] * value
            total[k] = total[k] + weight[m] * value
    half = 0.5 * occupied
    pull, by_weight, by_radius = [], [], []
    for m in each:
        bond_sum = jnp.maximum(total[m], 1.0)
        power = jnp.exp(expo_n * jnp.log(beta_t * bond_sum))
        bond = jnp.exp((-0.5 / expo_n) * jnp.log(1.0 + power))
        loss = 0.5 * bond * power / ((1.0 + power) * bond_sum)
        pull.append(half * weight[m] * attract[m] * loss * step_gate(total[m]))
        by_weight.append(half * (repulse[m] - attract[m] * bond))
        by_radius.append(
            half * weight[m] * (decay_two * attract[m] * bond - decay_one * repulse[m])
        )
    by_unit = [[zero] * 3 for _ in each]
    for m in each:
        for k in range(m + 1, entries):
            by_weight[m] = by_weight[m] + pull[k] * angular[m, k]
            by_weight[k] = by_weight[k] + pull[m] * angular[m, k]
            turn = (pull[m] * weight[k] + pull[k] * weight[m]) * tilt[m, k]
            for q in range(3):
                by_unit[m][q] = by_unit[m][q] + turn * unit[k][q]
                by_unit[k][q] = by_unit[k][q] + turn * unit[m][q]
    grads = []
    for m in each:
        across = [by_unit[m][q] * inverse[m] for q in range(3)]
        along = sum(across[q] * unit[m][q] for q in range(3))
        reach = gate_r[m] * (by_radius[m] + by_weight[m] * slope[m] - along)
        grads.append([across[q] + unit[m][q] * reach for q in range(3)])
    return grads


def force_kernel(
    rows, middle, got_a, got_b, got_c, got_d, lists, *refs, counts, cells_x, cells_y, capacity, turns
):
    outs = refs[: len(turns) + 1] if turns else refs[:1]
    table, index, parts, hot, left_side, main, ghost = refs[len(outs) :]
    entries, slots = lists.shape[0], lists.shape[3]
    shift = slots.bit_length() - 1
    at_x, at_y = lax.axis_index("gx"), lax.axis_index("gy")
    even_x, even_y = lax.rem(at_x, 2) == 0, lax.rem(at_y, 2) == 0
    wide, near = cells_x + 4, cells_x + 2
    centers = near * cells_y
    base = 4 * cells_x * cells_y
    for m in range(entries):
        here = pl.ds(base + m * cells_y, cells_y)
        left = jnp.where(even_x, got_b[here, :], got_a[here, :]).astype(jnp.int32)
        right = jnp.where(even_x, got_a[here, :], got_b[here, :]).astype(jnp.int32)
        for y in range(cells_y):
            index[m, pl.ds(y * near, 1), :] = left[y : y + 1]
            for x in range(cells_x):
                index[m, pl.ds(y * near + 1 + x, 1), :] = lists[m, x, pl.ds(y, 1), :]
            index[m, pl.ds(y * near + near - 1, 1), :] = right[y : y + 1]
    has_below, has_above = at_y > 0, at_y < counts[1] - 1
    strips = []
    for y in range(-1, cells_y + 1):
        if 0 <= y < cells_y:
            strip = [middle[q, y] for q in range(4)]
        else:
            swap, there = (even_y, has_below) if y < 0 else (jnp.logical_not(even_y), has_above)
            strip = [
                jnp.where(swap, got_d[pl.ds(q * wide, wide), :], got_c[pl.ds(q * wide, wide), :])
                for q in range(4)
            ]
            strip[3] = strip[3] * there.astype(jnp.float32)
        strip[2] = jnp.where(strip[3] > 0.0, strip[2], far_away)
        for move in range(3):
            for q in range(4):
                table[q, move, pl.ds((y + 1) * near, near), :] = strip[q][move : move + near]
    center = [table[q, 1, pl.ds(near, centers), :] for q in range(4)]
    occupied = center[3]
    entry_slot, entry_cell = [], []
    for m in range(entries):
        value = index[m]
        entry_slot.append(value & (slots - 1))
        entry_cell.append(value >> shift)
    nearby = [[None] * 3 for _ in range(entries)]
    for q in range(3):
        for c in range(9):
            source = table[q, c // 3, pl.ds((c % 3) * near, centers), :]
            for m in range(entries):
                picked = jnp.take_along_axis(
                    source, entry_slot[m], axis=1, mode="promise_in_bounds"
                )
                nearby[m][q] = (
                    picked if c == 0 else jnp.where(entry_cell[m] == c, picked, nearby[m][q])
                )
    grads = column_gradients(center[:3], occupied, nearby)
    own = [sum(grads[m][q] for m in range(entries)) for q in range(3)]
    for m in range(entries):
        index[m] = entry_slot[m]
        for q in range(3):
            high = grads[m][q].astype(jnp.bfloat16).astype(jnp.float32)
            parts[m, 3 + q] = high
            parts[m, q] = grads[m][q] - high
        parts[m, 6] = entry_cell[m].astype(jnp.float32)
        parts[m, 7] = jnp.zeros_like(occupied)
    for q in range(3):
        parts[entries, q] = jnp.zeros_like(occupied)
        parts[entries, 3 + q] = own[q]
    for q in (6, 7):
        parts[entries, q] = jnp.zeros_like(occupied)
    reached = {}
    ramp = lax.broadcasted_iota(jnp.int32, (slots, slots), 0)
    for y in range(cells_y):
        for x in range(-1, cells_x + 1):
            i = y * near + x + 1
            targets = [
                (dx, dy) for dx in (-1, 0, 1) if 0 <= x + dx < cells_x for dy in (-1, 0, 1)
            ]
            for m in range(entries):
                lanes = pl.ds(m * slots, slots)
                row = jnp.broadcast_to(index[m, pl.ds(i, 1), :], (slots, slots))
                hot[:, lanes] = jnp.where(ramp == row, 1.0, 0.0).astype(jnp.bfloat16)
                values = parts[m, :, i, :]
                cell = jnp.broadcast_to(parts[m, 6, pl.ds(i, 1), :], (ROWS, slots))
                masked = []
                for dx, dy in targets:
                    c = (dx + 1) * 3 + dy + 1
                    masked.append(jnp.where(cell == float(c), values, 0.0))
                left_side[pl.ds(0, ROWS * len(targets)), lanes] = jnp.concatenate(
                    masked, axis=0
                ).astype(jnp.bfloat16)
            sums = lax.dot_general(
                left_side[pl.ds(0, ROWS * len(targets)), :],
                hot[...],
                (((1,), (1,)), ((), ())),
                preferred_element_type=jnp.float32,
            )
            for n, (dx, dy) in enumerate(targets):
                key = (x + dx, y + dy)
                block = sums[n * ROWS : (n + 1) * ROWS]
                reached[key] = block if key not in reached else reached[key] + block
    line = lax.broadcasted_iota(jnp.int32, (ROWS, slots), 0)
    kick = half_step * force_scale
    chosen = (line >= 3) & (line < 6)
    for x in range(cells_x):
        for y in range(-1, cells_y + 1):
            block = reached[x, y]
            block = block + pltpu.roll(block, 3, 0)
            if 0 <= y < cells_y:
                block = parts[entries, :, y * near + x + 1, :] - block
                column = rows[pl.ds((x * cells_y + y) * ROWS, ROWS), :]
                column = column + jnp.where(chosen, kick * block, 0.0)
                main[x * cells_y + y] = column
            else:
                ghost[0 if y < 0 else 1, x] = -kick * block
    places = [4 * wide + x for x in range(cells_x)]
    below = [jnp.where(even_y, got_d[pl.ds(p, 1), :], got_c[pl.ds(p, 1), :]) for p in places]
    above = [jnp.where(even_y, got_c[pl.ds(p, 1), :], got_d[pl.ds(p, 1), :]) for p in places]
    columns = [main[c] for c in range(cells_x * cells_y)]
    named_here = [
        jnp.broadcast_to(main[c, pl.ds(7, 1), :], (ROWS, slots)) for c in range(cells_x * cells_y)
    ]

    def message(owner):
        pieces = []
        for slot in range(capacity):
            wanted = (owner * capacity + slot).astype(jnp.float32)
            piece = 0.0
            for column, named in zip(columns, named_here):
                piece = piece + jnp.where(named == wanted, column, 0.0)
            pieces.append(piece[:7])
        for side, named in enumerate((below, above)):
            for slot in range(capacity):
                wanted = (owner * capacity + slot).astype(jnp.float32)
                piece = 0.0
                for x in range(cells_x):
                    piece = piece + jnp.where(named[x] == wanted, ghost[side, x, pl.ds(3, 3), :], 0.0)
                pieces.append(piece)
        return pieces

    def write(ref, pieces):
        first = 0
        for piece in pieces:
            ref[pl.ds(first, piece.shape[0]), :] = piece
            first += piece.shape[0]

    if turns:
        for ref, turn in zip(outs[:-1], turns):
            write(ref, message(round_partner(at_y, turn, counts[1])))
        write(outs[-1], message(at_y))
    else:
        for owner in range(counts[1]):
            write(outs[0].at[owner], message(jnp.int32(owner)))


def gather_kernel(*refs, count, capacity, turns):
    at_y = lax.axis_index("gy")
    if turns:
        ins, out, held = refs[:-2], refs[-2], refs[-1]
        for ref, turn in zip(ins[:-1], turns):
            held[round_partner(at_y, turn, count)] = ref[...]
        held[at_y] = ins[-1][...]
    else:
        held, out = refs
    first = capacity * 7
    for source in range(count):
        for slot in range(capacity):
            block = held[source, pl.ds(slot * 7, 7), :]
            speed = block[3:6]
            if source + 1 < count:
                speed = speed + held[source + 1, pl.ds(first + slot * 3, 3), :]
            if source > 0:
                speed = speed + held[source - 1, pl.ds(first + (capacity + slot) * 3, 3), :]
            for line in range(7):
                value = speed[line - 3 : line - 2] if 3 <= line < 6 else block[line : line + 1]
                out[source, line, pl.ds(slot, 1), :] = value


def per_device(displacement, velocity, forces, heights, counts, neighbours, plan):
    cells_x, cells_y, slots = heights.shape
    entries = neighbours.shape[0]
    sizes = (lax.axis_size("gx"), lax.axis_size("gy"))
    columns = cells_x * cells_y
    capacity = max(2, (2 * columns + sizes[1] - 1) // sizes[1])
    inputs = (displacement, velocity, forces, heights, counts, neighbours, plan.reshape(1, columns))
    whole = pl.BlockSpec(memory_space=VMEM)
    shape = lambda *dims: jax.ShapeDtypeStruct(dims, jnp.float32)
    wide, near = cells_x + 4, cells_x + 2
    centers = near * cells_y

    def swap(value, pairs):
        return lax.ppermute(value, ("gx", "gy"), pairs)

    first_size = 4 * columns + entries * cells_y
    rows, send_a, send_b = pl.pallas_call(
        functools.partial(prepare_kernel, capacity=capacity),
        out_shape=(shape(columns * ROWS, slots), shape(first_size, slots), shape(first_size, slots)),
        in_specs=[pl.BlockSpec(memory_space=HBM)] * len(inputs),
        out_specs=(whole, whole, whole),
        scratch_shapes=[pltpu.VMEM(value.shape, value.dtype) for value in inputs]
        + [pltpu.SemaphoreType.DMA((len(inputs),))],
        compiler_params=pltpu.CompilerParams(vmem_limit_bytes=VMEM_BYTES),
        name="prepare",
    )(*[pltpu.with_memory_space_constraint(value, HBM) for value in inputs])
    got_a = swap(send_a, exchange_pairs(sizes, 0, False))
    got_b = swap(send_b, exchange_pairs(sizes, 0, True))
    second_size = 4 * wide + cells_x
    middle, send_c, send_d = pl.pallas_call(
        functools.partial(strip_kernel, count_x=sizes[0], cells_x=cells_x, cells_y=cells_y),
        out_shape=(shape(4, cells_y, wide, slots), shape(second_size, slots), shape(second_size, slots)),
        in_specs=[whole] * 4,
        out_specs=(whole, whole, whole),
        compiler_params=pltpu.CompilerParams(vmem_limit_bytes=VMEM_BYTES),
        name="strips",
    )(rows, send_a, got_a, got_b)
    got_c = swap(send_c, exchange_pairs(sizes, 1, False))
    got_d = swap(send_d, exchange_pairs(sizes, 1, True))
    turns = tuple(range(sizes[1] - 1)) if sizes[1] in (2, 4) else ()
    size = capacity * 13
    out_shape = (shape(size, slots),) * (len(turns) + 1) if turns else (shape(sizes[1], size, slots),)
    sent = pl.pallas_call(
        functools.partial(
            force_kernel, counts=sizes, cells_x=cells_x, cells_y=cells_y, capacity=capacity, turns=turns
        ),
        out_shape=out_shape,
        in_specs=[whole] * 7,
        out_specs=tuple(whole for _ in out_shape),
        scratch_shapes=[
            pltpu.VMEM((4, 3, near * (cells_y + 2), slots), jnp.float32),
            pltpu.VMEM((entries, centers, slots), jnp.int32),
            pltpu.VMEM((entries + 1, ROWS, centers, slots), jnp.float32),
            pltpu.VMEM((slots, entries * slots), jnp.bfloat16),
            pltpu.VMEM((9 * ROWS, entries * slots), jnp.bfloat16),
            pltpu.VMEM((columns, ROWS, slots), jnp.float32),
            pltpu.VMEM((2, cells_x, ROWS, slots), jnp.float32),
        ],
        compiler_params=pltpu.CompilerParams(vmem_limit_bytes=VMEM_BYTES),
        name="forces",
    )(rows, middle, got_a, got_b, got_c, got_d, neighbours)
    if turns:
        arrived = [swap(value, round_pairs(sizes, turn)) for value, turn in zip(sent, turns)]
        arrived.append(sent[-1])
        scratch = [pltpu.VMEM((sizes[1], size, slots), jnp.float32)]
    else:
        arrived = [lax.all_to_all(sent[0], "gy", split_axis=0, concat_axis=0, tiled=True)]
        scratch = []
    result = pl.pallas_call(
        functools.partial(gather_kernel, count=sizes[1], capacity=capacity, turns=turns),
        out_shape=shape(sizes[1], 7, capacity, slots),
        in_specs=[whole] * len(arrived),
        out_specs=whole,
        scratch_shapes=scratch,
        compiler_params=pltpu.CompilerParams(vmem_limit_bytes=VMEM_BYTES),
        name="collect",
    )(*arrived)
    return jnp.swapaxes(result, 1, 2)[None, None]


def solution(mesh):
    in_specs = (
        P(None, "gx", "gy", None),
        P(None, "gx", "gy", None),
        P(None, "gx", "gy", None),
        P("gx", "gy", None),
        P("gx", "gy"),
        P(None, "gx", "gy", None),
        P("gx", "gy", None, None),
    )
    out_specs = P("gx", "gy", None, None, None, None)
    return jax.shard_map(
        per_device, mesh=mesh, in_specs=in_specs, out_specs=out_specs, check_vma=False
    )
```

```python
import functools

import jax
import jax.numpy as jnp
from jax import lax
from jax.experimental import pallas as pl
from jax.experimental.pallas import tpu as pltpu
from jax.sharding import PartitionSpec as P

repulse_a = 1830.8
attract_b = 471.18
decay_one = 2.4799
decay_two = 1.7322
beta_t = 1.1e-06
expo_n = 0.78734
coeff_c2 = 100390.0**2
coeff_d2 = 16.217**2
coeff_h = -0.59825
spacing = 2.4
time_step = 0.001
half_step = 0.0005
force_scale = 9648.53 / 28.0855
far_away = 1.0e6
half_pi = 1.5707963267948966
VMEM_BYTES = 8 * 2**20
ROWS = 8

VMEM = pltpu.MemorySpace.VMEM
HBM = pltpu.MemorySpace.HBM


def line_partner(place, count, odd):
    other = ((place - 1) ^ 1) + 1 if odd else place ^ 1
    return other if 0 <= other < count else None


def exchange_pairs(counts, axis, odd):
    pairs = []
    for a in range(counts[0]):
        for b in range(counts[1]):
            here = [a, b]
            other = line_partner(here[axis], counts[axis], odd)
            if other is not None:
                here[axis] = other
            else:
                spare = line_partner(here[1 - axis], counts[1 - axis], False)
                if spare is None:
                    continue
                here[1 - axis] = spare
            pairs.append((a * counts[1] + b, here[0] * counts[1] + here[1]))
    return pairs


def round_partner(place, turn, count):
    ring = count - 1
    other = lax.rem(turn - place + 2 * ring, ring)
    alone = turn * ((ring + 1) // 2) % ring
    return jnp.where(place == ring, alone, jnp.where(place == alone, ring, other))


def round_pairs(counts, turn):
    ring = counts[1] - 1
    alone = turn * ((ring + 1) // 2) % ring
    pairs = []
    for a in range(counts[0]):
        for b in range(counts[1]):
            other = alone if b == ring else ring if b == alone else (turn - b) % ring
            pairs.append((a * counts[1] + b, a * counts[1] + other))
    return pairs


def prepare_kernel(*refs, capacity):
    count = 7
    sources, (rows, send_a, send_b) = refs[:count], refs[count : count + 3]
    held, done = refs[count + 3 : -1], refs[-1]
    copies = [
        pltpu.make_async_copy(source, target, done.at[n])
        for n, (source, target) in enumerate(zip(sources, held))
    ]
    for copy in copies:
        copy.start()
    disp, vel, force, heights, counts, lists, plan = held
    _, cells_x, cells_y, slots = disp.shape
    entries = lists.shape[0]
    at_x, at_y = lax.axis_index("gx"), lax.axis_index("gy")
    even_x = lax.rem(at_x, 2) == 0
    for copy in copies:
        copy.wait()
    owners = [plan[:, c : c + 1] for c in range(cells_x * cells_y)]
    for x in range(cells_x):
        base_x = ((at_x * cells_x + x).astype(jnp.float32) + 0.5) * spacing
        for y in range(cells_y):
            base_y = ((at_y * cells_y + y).astype(jnp.float32) + 0.5) * spacing
            layer = heights[x, pl.ds(y, 1), :]
            occupied = (layer < counts[x : x + 1, y : y + 1]).astype(jnp.float32)
            lattice = (base_x, base_y, (layer.astype(jnp.float32) + 0.5) * spacing)
            column = (x * cells_y + y) * ROWS
            for q in range(3):
                pick = (q, x, pl.ds(y, 1), slice(None))
                speed = vel[pick] + half_step * (force[pick] * force_scale)
                offset = disp[pick] + time_step * speed
                rows[pl.ds(column + q, 1), :] = offset
                rows[pl.ds(column + 3 + q, 1), :] = speed
                point = lattice[q] + offset
                place = (q * cells_y + y) * cells_x + x
                send_a[pl.ds(place, 1), :] = point
                send_b[pl.ds(place, 1), :] = point
            rows[pl.ds(column + 6, 1), :] = occupied
            owner = owners[x * cells_y + y]
            earlier = sum((owners[c] == owner).astype(jnp.int32) for c in range(x * cells_y + y))
            rows[pl.ds(column + 7, 1), :] = jnp.broadcast_to(
                (owner * capacity + earlier).astype(jnp.float32), (1, slots)
            )
            place = (3 * cells_y + y) * cells_x + x
            send_a[pl.ds(place, 1), :] = occupied
            send_b[pl.ds(place, 1), :] = occupied
    base = 4 * cells_y * cells_x
    for m in range(entries):
        low = lists[m, 0].astype(jnp.float32)
        high = lists[m, cells_x - 1].astype(jnp.float32)
        send_a[pl.ds(base + m * cells_y, cells_y), :] = jnp.where(even_x, high, low)
        send_b[pl.ds(base + m * cells_y, cells_y), :] = jnp.where(even_x, low, high)


def strip_kernel(rows, own, got_a, got_b, middle, send_c, send_d, *, count_x, cells_x, cells_y):
    at_x, at_y = lax.axis_index("gx"), lax.axis_index("gy")
    even_x, even_y = lax.rem(at_x, 2) == 0, lax.rem(at_y, 2) == 0
    has_left = (at_x > 0).astype(jnp.float32)
    has_right = (at_x < count_x - 1).astype(jnp.float32)
    wide = cells_x + 4
    for q in range(4):
        for y in range(cells_y):
            place = (q * cells_y + y) * cells_x
            take = lambda ref: ref[pl.ds(place, cells_x), :]
            left = jnp.where(even_x, take(got_b), take(got_a))[cells_x - 2 :]
            right = jnp.where(even_x, take(got_a), take(got_b))[:2]
            if q == 3:
                left, right = left * has_left, right * has_right
            strip = jnp.concatenate([left, take(own), right], axis=0)
            middle[q, y] = strip
        low, high = middle[q, 0], middle[q, cells_y - 1]
        send_c[pl.ds(q * wide, wide), :] = jnp.where(even_y, high, low)
        send_d[pl.ds(q * wide, wide), :] = jnp.where(even_y, low, high)
    for x in range(cells_x):
        low = rows[pl.ds(x * cells_y * ROWS + 7, 1), :]
        high = rows[pl.ds((x * cells_y + cells_y - 1) * ROWS + 7, 1), :]
        send_c[pl.ds(4 * wide + x, 1), :] = jnp.where(even_y, high, low)
        send_d[pl.ds(4 * wide + x, 1), :] = jnp.where(even_y, low, high)


def half_wave(radius):
    angle = half_pi * (jnp.clip(radius, 2.7, 3.0) - 2.85) / 0.15
    square = angle * angle
    sine, cosine = 0.0, 0.0
    for odd in (15, 13, 11, 9, 7, 5, 3, 1):
        factor_s = 1.0
        for n in range(2, odd + 1):
            factor_s /= n
        factor_c = factor_s * odd
        sign = -1.0 if odd % 4 == 3 else 1.0
        sine = sine * square + sign * factor_s
        cosine = cosine * square + sign * factor_c
    return sine * angle, cosine


def step_gate(value):
    return jnp.where(value > 1.0, 1.0, jnp.where(value == 1.0, 0.5, 0.0))


def column_gradients(center, occupied, nearby):
    entries = len(nearby)
    each = range(entries)
    inverse, gate_r, weight, slope, unit, repulse, attract = [], [], [], [], [], [], []
    for m in each:
        offset = [nearby[m][q] - center[q] for q in range(3)]
        square = offset[0] * offset[0] + offset[1] * offset[1] + offset[2] * offset[2]
        bounded = jnp.maximum(square, 1.0)
        radius = jnp.sqrt(bounded)
        inverse.append(1.0 / radius)
        gate_r.append(step_gate(square))
        sine, cosine = half_wave(radius)
        inside, outside = radius < 2.7, radius > 3.0
        weight.append(jnp.where(inside, 1.0, jnp.where(outside, 0.0, 0.5 - 0.5 * sine)))
        slope.append(jnp.where(inside | outside, 0.0, (-0.5 * half_pi / 0.15) * cosine))
        unit.append([offset[q] * inverse[m] for q in range(3)])
        repulse.append(repulse_a * jnp.exp(-decay_one * radius))
        attract.append(attract_b * jnp.exp(-decay_two * radius))
    zero = jnp.zeros_like(occupied)
    total = [zero for _ in each]
    angular, tilt = {}, {}
    for m in each:
        for k in range(m + 1, entries):
            cosine = sum(unit[m][q] * unit[k][q] for q in range(3))
            lean = coeff_h - cosine
            spread = lean * lean
            part = 1.0 / (coeff_d2 + spread)
            value = 1.0 + (coeff_c2 / coeff_d2) * (spread * part)
            angular[m, k] = value
            tilt[m, k] = (-2.0 * coeff_c2) * lean * (part * part)
            total[m] = total[m] + weight[k] * value
            total[k] = total[k] + weight[m] * value
    half = 0.5 * occupied
    pull, by_weight, by_radius = [], [], []
    for m in each:
        bond_sum = jnp.maximum(total[m], 1.0)
        power = jnp.exp(expo_n * jnp.log(beta_t * bond_sum))
        bond = jnp.exp((-0.5 / expo_n) * jnp.log(1.0 + power))
        loss = 0.5 * bond * power / ((1.0 + power) * bond_sum)
        pull.append(half * weight[m] * attract[m] * loss * step_gate(total[m]))
        by_weight.append(half * (repulse[m] - attract[m] * bond))
        by_radius.append(
            half * weight[m] * (decay_two * attract[m] * bond - decay_one * repulse[m])
        )
    by_unit = [[zero] * 3 for _ in each]
    for m in each:
        for k in range(m + 1, entries):
            by_weight[m] = by_weight[m] + pull[k] * angular[m, k]
            by_weight[k] = by_weight[k] + pull[m] * angular[m, k]
            turn = (pull[m] * weight[k] + pull[k] * weight[m]) * tilt[m, k]
            for q in range(3):
                by_unit[m][q] = by_unit[m][q] + turn * unit[k][q]
                by_unit[k][q] = by_unit[k][q] + turn * unit[m][q]
    grads = []
    for m in each:
        across = [by_unit[m][q] * inverse[m] for q in range(3)]
        along = sum(across[q] * unit[m][q] for q in range(3))
        reach = gate_r[m] * (by_radius[m] + by_weight[m] * slope[m] - along)
        grads.append([across[q] + unit[m][q] * reach for q in range(3)])
    return grads


def near_kernel(
    middle, got_a, got_b, lists, centre, nearby, slot_at, cell_at, spots, cells, table, index, *, cells_x, cells_y
):
    entries, slots = lists.shape[0], lists.shape[3]
    shift = slots.bit_length() - 1
    even_x = lax.rem(lax.axis_index("gx"), 2) == 0
    near = cells_x + 2
    centers = near * cells_y
    base = 4 * cells_x * cells_y
    for m in range(entries):
        here = pl.ds(base + m * cells_y, cells_y)
        left = jnp.where(even_x, got_b[here, :], got_a[here, :]).astype(jnp.int32)
        right = jnp.where(even_x, got_a[here, :], got_b[here, :]).astype(jnp.int32)
        for y in range(cells_y):
            index[m, pl.ds(y * near, 1), :] = left[y : y + 1]
            for x in range(cells_x):
                index[m, pl.ds(y * near + 1 + x, 1), :] = lists[m, x, pl.ds(y, 1), :]
            index[m, pl.ds(y * near + near - 1, 1), :] = right[y : y + 1]
    for y in range(cells_y):
        strip = [middle[q, y] for q in range(4)]
        centre[3, pl.ds(y * near, near), :] = strip[3][1 : 1 + near]
        strip[2] = jnp.where(strip[3] > 0.0, strip[2], far_away)
        for q in range(3):
            for move in range(3):
                table[q, move, pl.ds((y + 1) * near, near), :] = strip[q][move : move + near]
    for q in range(3):
        for move in range(3):
            for y in (0, cells_y + 1):
                table[q, move, pl.ds(y * near, near), :] = jnp.zeros((near, slots), jnp.float32)
        centre[q] = table[q, 1, pl.ds(near, centers), :]
    line = lax.broadcasted_iota(jnp.int32, (centers, slots), 0)
    for m in range(entries):
        value = index[m]
        slot, cell = value & (slots - 1), value >> shift
        picked = []
        for c in range(9):
            for q in range(3):
                source = table[q, c // 3, pl.ds((c % 3) * near, centers), :]
                got = jnp.take_along_axis(source, slot, axis=1, mode="promise_in_bounds")
                if c == 0:
                    picked.append(got)
                else:
                    picked[q] = jnp.where(cell == c, got, picked[q])
        for q in range(3):
            nearby[m, q] = picked[q]
        move_x = jnp.where(cell < 3, 0, jnp.where(cell < 6, 1, 2))
        move_y = cell - 3 * move_x
        away = ((line < near) & (move_y == 0)) | ((line >= centers - near) & (move_y == 2))
        slot_at[m] = slot
        cell_at[m] = jnp.where(away, move_x, 3)
        spots[pl.ds(m * centers, centers), :] = slot.astype(jnp.float32)
        cells[pl.ds(m * centers, centers), :] = cell.astype(jnp.float32)


def force_kernel(
    rows, centre, nearby_own, slot_at, cell_at, spots, cells, got_c, got_d, *refs,
    counts, cells_x, cells_y, capacity, turns
):
    outs = refs[: len(turns) + 1] if turns else refs[:1]
    table, parts, main, ghost = refs[len(outs) :]
    entries, centers, slots = slot_at.shape
    at_y = lax.axis_index("gy")
    even_y = lax.rem(at_y, 2) == 0
    wide, near = cells_x + 4, cells_x + 2
    has_below, has_above = at_y > 0, at_y < counts[1] - 1
    for row, swap, there in (
        (0, even_y, has_below),
        (centers - near, jnp.logical_not(even_y), has_above),
    ):
        strip = [
            jnp.where(swap, got_d[pl.ds(q * wide, wide), :], got_c[pl.ds(q * wide, wide), :])
            for q in range(4)
        ]
        full = strip[3] * there.astype(jnp.float32) > 0.0
        strip[2] = jnp.where(full, strip[2], far_away)
        for move in range(3):
            for q in range(3):
                table[q, move, pl.ds(row, near), :] = strip[q][move : move + near]
    for y in range(1, cells_y - 1):
        for move in range(3):
            for q in range(3):
                table[q, move, pl.ds(y * near, near), :] = jnp.zeros((near, slots), jnp.float32)
    center = [centre[q] for q in range(3)]
    occupied = centre[3]
    nearby = []
    for m in range(entries):
        picked = [nearby_own[m, q] for q in range(3)]
        slot, cell = slot_at[m], cell_at[m]
        for move in range(3):
            for q in range(3):
                got = jnp.take_along_axis(table[q, move], slot, axis=1, mode="promise_in_bounds")
                picked[q] = jnp.where(cell == move, got, picked[q])
        nearby.append(picked)
    grads = column_gradients(center, occupied, nearby)
    own = [sum(grads[m][q] for m in range(entries)) for q in range(3)]
    zero = jnp.zeros_like(occupied)

    def part(m, row):
        return pl.ds((m * ROWS + row) * centers, centers)

    def column_parts(m, i):
        return parts[pl.ds(m * ROWS * centers + i, ROWS, stride=centers), :]

    for m in range(entries):
        for q in range(3):
            high = grads[m][q].astype(jnp.bfloat16).astype(jnp.float32)
            parts[part(m, 3 + q), :] = high
            parts[part(m, q), :] = grads[m][q] - high
        for row in (6, 7):
            parts[part(m, row), :] = zero
    for q in range(3):
        parts[part(entries, 3 + q), :] = own[q]
    for row in (0, 1, 2, 6, 7):
        parts[part(entries, row), :] = zero
    reached = {}
    step = 16
    ramps = [
        (lax.broadcasted_iota(jnp.int32, (step, slots), 0) + first).astype(jnp.float32).astype(jnp.bfloat16)
        for first in range(0, slots, step)
    ]
    one, none = jnp.ones((step, slots), jnp.bfloat16), jnp.zeros((step, slots), jnp.bfloat16)
    for y in range(cells_y):
        for x in range(-1, cells_x + 1):
            i = y * near + x + 1
            targets = [
                (dx, dy) for dx in (-1, 0, 1) if 0 <= x + dx < cells_x for dy in (-1, 0, 1)
            ]
            hot, left_side = [], []
            for m in range(entries):
                row = spots[pl.ds(m * centers + i, step, stride=0), :].astype(jnp.bfloat16)
                hot.append(
                    jnp.concatenate([jnp.where(ramp == row, one, none) for ramp in ramps], axis=0)
                )
                values = column_parts(m, i)
                cell = cells[pl.ds(m * centers + i, ROWS, stride=0), :]
                masked = [
                    jnp.where(cell == float((dx + 1) * 3 + dy + 1), values, 0.0) for dx, dy in targets
                ]
                left_side.append(jnp.concatenate(masked, axis=0).astype(jnp.bfloat16))
            sums = lax.dot_general(
                jnp.concatenate(left_side, axis=1),
                jnp.concatenate(hot, axis=1),
                (((1,), (1,)), ((), ())),
                preferred_element_type=jnp.float32,
            )
            for n, (dx, dy) in enumerate(targets):
                key = (x + dx, y + dy)
                block = sums[n * ROWS : (n + 1) * ROWS]
                reached[key] = block if key not in reached else reached[key] + block
    line = lax.broadcasted_iota(jnp.int32, (ROWS, slots), 0)
    kick = half_step * force_scale
    chosen = (line >= 3) & (line < 6)
    for x in range(cells_x):
        for y in range(-1, cells_y + 1):
            block = reached[x, y]
            block = block + pltpu.roll(block, 3, 0)
            if 0 <= y < cells_y:
                block = column_parts(entries, y * near + x + 1) - block
                column = rows[pl.ds((x * cells_y + y) * ROWS, ROWS), :]
                column = column + jnp.where(chosen, kick * block, 0.0)
                main[x * cells_y + y] = column
            else:
                ghost[0 if y < 0 else 1, x] = -kick * block
    places = [4 * wide + x for x in range(cells_x)]
    below = [jnp.where(even_y, got_d[pl.ds(p, 1), :], got_c[pl.ds(p, 1), :]) for p in places]
    above = [jnp.where(even_y, got_c[pl.ds(p, 1), :], got_d[pl.ds(p, 1), :]) for p in places]
    columns = [main[c] for c in range(cells_x * cells_y)]
    named_here = [
        jnp.broadcast_to(main[c, pl.ds(7, 1), :], (ROWS, slots)) for c in range(cells_x * cells_y)
    ]

    def message(owner):
        pieces = []
        for slot in range(capacity):
            wanted = (owner * capacity + slot).astype(jnp.float32)
            piece = 0.0
            for column, named in zip(columns, named_here):
                piece = piece + jnp.where(named == wanted, column, 0.0)
            pieces.append(piece[:7])
        for side, named in enumerate((below, above)):
            for slot in range(capacity):
                wanted = (owner * capacity + slot).astype(jnp.float32)
                piece = 0.0
                for x in range(cells_x):
                    piece = piece + jnp.where(named[x] == wanted, ghost[side, x, pl.ds(3, 3), :], 0.0)
                pieces.append(piece)
        return pieces

    def write(ref, pieces):
        first = 0
        for piece in pieces:
            ref[pl.ds(first, piece.shape[0]), :] = piece
            first += piece.shape[0]

    if turns:
        for ref, turn in zip(outs[:-1], turns):
            write(ref, message(round_partner(at_y, turn, counts[1])))
        write(outs[-1], message(at_y))
    else:
        for owner in range(counts[1]):
            write(outs[0].at[owner], message(jnp.int32(owner)))


def gather_kernel(*refs, count, capacity, turns):
    at_y = lax.axis_index("gy")
    if turns:
        ins, out, held = refs[:-2], refs[-2], refs[-1]
        for ref, turn in zip(ins[:-1], turns):
            held[round_partner(at_y, turn, count)] = ref[...]
        held[at_y] = ins[-1][...]
    else:
        held, out = refs
    first = capacity * 7
    for source in range(count):
        for slot in range(capacity):
            block = held[source, pl.ds(slot * 7, 7), :]
            speed = block[3:6]
            if source + 1 < count:
                speed = speed + held[source + 1, pl.ds(first + slot * 3, 3), :]
            if source > 0:
                speed = speed + held[source - 1, pl.ds(first + (capacity + slot) * 3, 3), :]
            for line in range(7):
                value = speed[line - 3 : line - 2] if 3 <= line < 6 else block[line : line + 1]
                out[source, line, pl.ds(slot, 1), :] = value


def per_device(displacement, velocity, forces, heights, counts, neighbours, plan):
    cells_x, cells_y, slots = heights.shape
    entries = neighbours.shape[0]
    sizes = (lax.axis_size("gx"), lax.axis_size("gy"))
    columns = cells_x * cells_y
    capacity = max(2, (2 * columns + sizes[1] - 1) // sizes[1])
    inputs = (displacement, velocity, forces, heights, counts, neighbours, plan.reshape(1, columns))
    whole = pl.BlockSpec(memory_space=VMEM)
    shape = lambda *dims: jax.ShapeDtypeStruct(dims, jnp.float32)
    wide, near = cells_x + 4, cells_x + 2
    centers = near * cells_y

    def swap(value, pairs):
        return lax.ppermute(value, ("gx", "gy"), pairs)

    first_size = 4 * columns + entries * cells_y
    rows, send_a, send_b = pl.pallas_call(
        functools.partial(prepare_kernel, capacity=capacity),
        out_shape=(shape(columns * ROWS, slots), shape(first_size, slots), shape(first_size, slots)),
        in_specs=[pl.BlockSpec(memory_space=HBM)] * len(inputs),
        out_specs=(whole, whole, whole),
        scratch_shapes=[pltpu.VMEM(value.shape, value.dtype) for value in inputs]
        + [pltpu.SemaphoreType.DMA((len(inputs),))],
        compiler_params=pltpu.CompilerParams(vmem_limit_bytes=VMEM_BYTES),
        name="prepare",
    )(*[pltpu.with_memory_space_constraint(value, HBM) for value in inputs])
    got_a = swap(send_a, exchange_pairs(sizes, 0, False))
    got_b = swap(send_b, exchange_pairs(sizes, 0, True))
    second_size = 4 * wide + cells_x
    middle, send_c, send_d = pl.pallas_call(
        functools.partial(strip_kernel, count_x=sizes[0], cells_x=cells_x, cells_y=cells_y),
        out_shape=(shape(4, cells_y, wide, slots), shape(second_size, slots), shape(second_size, slots)),
        in_specs=[whole] * 4,
        out_specs=(whole, whole, whole),
        compiler_params=pltpu.CompilerParams(vmem_limit_bytes=VMEM_BYTES),
        name="strips",
    )(rows, send_a, got_a, got_b)
    got_c = swap(send_c, exchange_pairs(sizes, 1, False))
    got_d = swap(send_d, exchange_pairs(sizes, 1, True))
    turns = tuple(range(sizes[1] - 1)) if sizes[1] in (2, 4) else ()
    size = capacity * 13
    out_shape = (shape(size, slots),) * (len(turns) + 1) if turns else (shape(sizes[1], size, slots),)
    flat = lambda kind, *dims: jax.ShapeDtypeStruct(dims, kind)
    found = pl.pallas_call(
        functools.partial(near_kernel, cells_x=cells_x, cells_y=cells_y),
        out_shape=(
            shape(4, centers, slots),
            shape(entries, 3, centers, slots),
            flat(jnp.int32, entries, centers, slots),
            flat(jnp.int32, entries, centers, slots),
            shape(entries * centers, slots),
            shape(entries * centers, slots),
        ),
        in_specs=[whole] * 4,
        out_specs=(whole,) * 6,
        scratch_shapes=[
            pltpu.VMEM((3, 3, near * (cells_y + 2), slots), jnp.float32),
            pltpu.VMEM((entries, centers, slots), jnp.int32),
        ],
        compiler_params=pltpu.CompilerParams(vmem_limit_bytes=VMEM_BYTES),
        cost_estimate=pl.CostEstimate(flops=1000000, bytes_accessed=200000, transcendentals=0),
        name="near",
    )(middle, got_a, got_b, neighbours)
    sent = pl.pallas_call(
        functools.partial(
            force_kernel, counts=sizes, cells_x=cells_x, cells_y=cells_y, capacity=capacity, turns=turns
        ),
        out_shape=out_shape,
        in_specs=[whole] * 9,
        out_specs=tuple(whole for _ in out_shape),
        scratch_shapes=[
            pltpu.VMEM((3, 3, centers, slots), jnp.float32),
            pltpu.VMEM(((entries + 1) * ROWS * centers, slots), jnp.float32),
            pltpu.VMEM((columns, ROWS, slots), jnp.float32),
            pltpu.VMEM((2, cells_x, ROWS, slots), jnp.float32),
        ],
        compiler_params=pltpu.CompilerParams(vmem_limit_bytes=VMEM_BYTES),
        name="forces",
    )(rows, *found, got_c, got_d)
    if turns:
        arrived = [swap(value, round_pairs(sizes, turn)) for value, turn in zip(sent, turns)]
        arrived.append(sent[-1])
        scratch = [pltpu.VMEM((sizes[1], size, slots), jnp.float32)]
    else:
        arrived = [lax.all_to_all(sent[0], "gy", split_axis=0, concat_axis=0, tiled=True)]
        scratch = []
    result = pl.pallas_call(
        functools.partial(gather_kernel, count=sizes[1], capacity=capacity, turns=turns),
        out_shape=shape(sizes[1], 7, capacity, slots),
        in_specs=[whole] * len(arrived),
        out_specs=whole,
        scratch_shapes=scratch,
        compiler_params=pltpu.CompilerParams(vmem_limit_bytes=VMEM_BYTES),
        name="collect",
    )(*arrived)
    return jnp.swapaxes(result, 1, 2)[None, None]


def solution(mesh):
    in_specs = (
        P(None, "gx", "gy", None),
        P(None, "gx", "gy", None),
        P(None, "gx", "gy", None),
        P("gx", "gy", None),
        P("gx", "gy"),
        P(None, "gx", "gy", None),
        P("gx", "gy", None, None),
    )
    out_specs = P("gx", "gy", None, None, None, None)
    return jax.shard_map(
        per_device, mesh=mesh, in_specs=in_specs, out_specs=out_specs, check_vma=False
    )
```

```python
import functools

import jax
import jax.numpy as jnp
from jax import lax
from jax.experimental import pallas as pl
from jax.experimental.pallas import tpu as pltpu
from jax.sharding import PartitionSpec as P

repulse_a = 1830.8
attract_b = 471.18
decay_one = 2.4799
decay_two = 1.7322
beta_t = 1.1e-06
expo_n = 0.78734
coeff_c2 = 100390.0**2
coeff_d2 = 16.217**2
coeff_h = -0.59825
spacing = 2.4
time_step = 0.001
half_step = 0.0005
force_scale = 9648.53 / 28.0855
far_away = 1.0e6
half_pi = 1.5707963267948966
VMEM_BYTES = 8 * 2**20
ROWS = 8

VMEM = pltpu.MemorySpace.VMEM
HBM = pltpu.MemorySpace.HBM


def line_partner(place, count, odd):
    other = ((place - 1) ^ 1) + 1 if odd else place ^ 1
    return other if 0 <= other < count else None


def exchange_pairs(counts, axis, odd):
    pairs = []
    for a in range(counts[0]):
        for b in range(counts[1]):
            here = [a, b]
            other = line_partner(here[axis], counts[axis], odd)
            if other is not None:
                here[axis] = other
            else:
                spare = line_partner(here[1 - axis], counts[1 - axis], False)
                if spare is None:
                    continue
                here[1 - axis] = spare
            pairs.append((a * counts[1] + b, here[0] * counts[1] + here[1]))
    return pairs


def round_partner(place, turn, count):
    ring = count - 1
    other = lax.rem(turn - place + 2 * ring, ring)
    alone = turn * ((ring + 1) // 2) % ring
    return jnp.where(place == ring, alone, jnp.where(place == alone, ring, other))


def round_pairs(counts, turn):
    ring = counts[1] - 1
    alone = turn * ((ring + 1) // 2) % ring
    pairs = []
    for a in range(counts[0]):
        for b in range(counts[1]):
            other = alone if b == ring else ring if b == alone else (turn - b) % ring
            pairs.append((a * counts[1] + b, a * counts[1] + other))
    return pairs


def prepare_kernel(*refs, capacity):
    count = 7
    sources, (rows, send_a, send_b) = refs[:count], refs[count : count + 3]
    held, done = refs[count + 3 : -1], refs[-1]
    copies = [
        pltpu.make_async_copy(source, target, done.at[n])
        for n, (source, target) in enumerate(zip(sources, held))
    ]
    for copy in copies:
        copy.start()
    disp, vel, force, heights, counts, lists, plan = held
    _, cells_x, cells_y, slots = disp.shape
    entries = lists.shape[0]
    at_x, at_y = lax.axis_index("gx"), lax.axis_index("gy")
    even_x = lax.rem(at_x, 2) == 0
    for copy in copies:
        copy.wait()
    owners = [plan[:, c : c + 1] for c in range(cells_x * cells_y)]
    for x in range(cells_x):
        base_x = ((at_x * cells_x + x).astype(jnp.float32) + 0.5) * spacing
        for y in range(cells_y):
            base_y = ((at_y * cells_y + y).astype(jnp.float32) + 0.5) * spacing
            layer = heights[x, pl.ds(y, 1), :]
            occupied = (layer < counts[x : x + 1, y : y + 1]).astype(jnp.float32)
            lattice = (base_x, base_y, (layer.astype(jnp.float32) + 0.5) * spacing)
            column = (x * cells_y + y) * ROWS
            for q in range(3):
                pick = (q, x, pl.ds(y, 1), slice(None))
                speed = vel[pick] + half_step * (force[pick] * force_scale)
                offset = disp[pick] + time_step * speed
                rows[pl.ds(column + q, 1), :] = offset
                rows[pl.ds(column + 3 + q, 1), :] = speed
                point = lattice[q] + offset
                place = (q * cells_y + y) * cells_x + x
                send_a[pl.ds(place, 1), :] = point
                send_b[pl.ds(place, 1), :] = point
            rows[pl.ds(column + 6, 1), :] = occupied
            owner = owners[x * cells_y + y]
            earlier = sum((owners[c] == owner).astype(jnp.int32) for c in range(x * cells_y + y))
            rows[pl.ds(column + 7, 1), :] = jnp.broadcast_to(
                (owner * capacity + earlier).astype(jnp.float32), (1, slots)
            )
            place = (3 * cells_y + y) * cells_x + x
            send_a[pl.ds(place, 1), :] = occupied
            send_b[pl.ds(place, 1), :] = occupied
    base = 4 * cells_y * cells_x
    for m in range(entries):
        low = lists[m, 0].astype(jnp.float32)
        high = lists[m, cells_x - 1].astype(jnp.float32)
        send_a[pl.ds(base + m * cells_y, cells_y), :] = jnp.where(even_x, high, low)
        send_b[pl.ds(base + m * cells_y, cells_y), :] = jnp.where(even_x, low, high)


def strip_kernel(rows, own, got_a, got_b, middle, send_c, send_d, *, count_x, cells_x, cells_y):
    at_x, at_y = lax.axis_index("gx"), lax.axis_index("gy")
    even_x, even_y = lax.rem(at_x, 2) == 0, lax.rem(at_y, 2) == 0
    has_left = (at_x > 0).astype(jnp.float32)
    has_right = (at_x < count_x - 1).astype(jnp.float32)
    wide = cells_x + 4
    for q in range(4):
        for y in range(cells_y):
            place = (q * cells_y + y) * cells_x
            take = lambda ref: ref[pl.ds(place, cells_x), :]
            left = jnp.where(even_x, take(got_b), take(got_a))[cells_x - 2 :]
            right = jnp.where(even_x, take(got_a), take(got_b))[:2]
            if q == 3:
                left, right = left * has_left, right * has_right
            strip = jnp.concatenate([left, take(own), right], axis=0)
            middle[q, y] = strip
        low, high = middle[q, 0], middle[q, cells_y - 1]
        send_c[pl.ds(q * wide, wide), :] = jnp.where(even_y, high, low)
        send_d[pl.ds(q * wide, wide), :] = jnp.where(even_y, low, high)
    for x in range(cells_x):
        low = rows[pl.ds(x * cells_y * ROWS + 7, 1), :]
        high = rows[pl.ds((x * cells_y + cells_y - 1) * ROWS + 7, 1), :]
        send_c[pl.ds(4 * wide + x, 1), :] = jnp.where(even_y, high, low)
        send_d[pl.ds(4 * wide + x, 1), :] = jnp.where(even_y, low, high)


def half_wave(radius):
    angle = half_pi * (jnp.clip(radius, 2.7, 3.0) - 2.85) / 0.15
    square = angle * angle
    sine, cosine = 0.0, 0.0
    for odd in (15, 13, 11, 9, 7, 5, 3, 1):
        factor_s = 1.0
        for n in range(2, odd + 1):
            factor_s /= n
        factor_c = factor_s * odd
        sign = -1.0 if odd % 4 == 3 else 1.0
        sine = sine * square + sign * factor_s
        cosine = cosine * square + sign * factor_c
    return sine * angle, cosine


def step_gate(value):
    return jnp.where(value > 1.0, 1.0, jnp.where(value == 1.0, 0.5, 0.0))


def column_gradients(center, occupied, nearby):
    entries = len(nearby)
    each = range(entries)
    inverse, gate_r, weight, slope, unit, repulse, attract = [], [], [], [], [], [], []
    for m in each:
        offset = [nearby[m][q] - center[q] for q in range(3)]
        square = offset[0] * offset[0] + offset[1] * offset[1] + offset[2] * offset[2]
        bounded = jnp.maximum(square, 1.0)
        radius = jnp.sqrt(bounded)
        inverse.append(1.0 / radius)
        gate_r.append(step_gate(square))
        sine, cosine = half_wave(radius)
        inside, outside = radius < 2.7, radius > 3.0
        weight.append(jnp.where(inside, 1.0, jnp.where(outside, 0.0, 0.5 - 0.5 * sine)))
        slope.append(jnp.where(inside | outside, 0.0, (-0.5 * half_pi / 0.15) * cosine))
        unit.append([offset[q] * inverse[m] for q in range(3)])
        repulse.append(repulse_a * jnp.exp(-decay_one * radius))
        attract.append(attract_b * jnp.exp(-decay_two * radius))
    zero = jnp.zeros_like(occupied)
    total = [zero for _ in each]
    angular, tilt = {}, {}
    for m in each:
        for k in range(m + 1, entries):
            cosine = sum(unit[m][q] * unit[k][q] for q in range(3))
            lean = coeff_h - cosine
            spread = lean * lean
            part = 1.0 / (coeff_d2 + spread)
            value = 1.0 + (coeff_c2 / coeff_d2) * (spread * part)
            angular[m, k] = value
            tilt[m, k] = (-2.0 * coeff_c2) * lean * (part * part)
            total[m] = total[m] + weight[k] * value
            total[k] = total[k] + weight[m] * value
    half = 0.5 * occupied
    pull, by_weight, by_radius = [], [], []
    for m in each:
        bond_sum = jnp.maximum(total[m], 1.0)
        power = jnp.exp(expo_n * jnp.log(beta_t * bond_sum))
        bond = jnp.exp((-0.5 / expo_n) * jnp.log(1.0 + power))
        loss = 0.5 * bond * power / ((1.0 + power) * bond_sum)
        pull.append(half * weight[m] * attract[m] * loss * step_gate(total[m]))
        by_weight.append(half * (repulse[m] - attract[m] * bond))
        by_radius.append(
            half * weight[m] * (decay_two * attract[m] * bond - decay_one * repulse[m])
        )
    by_unit = [[zero] * 3 for _ in each]
    for m in each:
        for k in range(m + 1, entries):
            by_weight[m] = by_weight[m] + pull[k] * angular[m, k]
            by_weight[k] = by_weight[k] + pull[m] * angular[m, k]
            turn = (pull[m] * weight[k] + pull[k] * weight[m]) * tilt[m, k]
            for q in range(3):
                by_unit[m][q] = by_unit[m][q] + turn * unit[k][q]
                by_unit[k][q] = by_unit[k][q] + turn * unit[m][q]
    grads = []
    for m in each:
        across = [by_unit[m][q] * inverse[m] for q in range(3)]
        along = sum(across[q] * unit[m][q] for q in range(3))
        reach = gate_r[m] * (by_radius[m] + by_weight[m] * slope[m] - along)
        grads.append([across[q] + unit[m][q] * reach for q in range(3)])
    return grads


def near_kernel(
    middle, got_a, got_b, lists, centre, nearby, slot_at, cell_at, spots, cells, table, index, *, cells_x, cells_y
):
    entries, slots = lists.shape[0], lists.shape[3]
    shift = slots.bit_length() - 1
    even_x = lax.rem(lax.axis_index("gx"), 2) == 0
    near = cells_x + 2
    centers = near * cells_y
    base = 4 * cells_x * cells_y
    for m in range(entries):
        here = pl.ds(base + m * cells_y, cells_y)
        left = jnp.where(even_x, got_b[here, :], got_a[here, :]).astype(jnp.int32)
        right = jnp.where(even_x, got_a[here, :], got_b[here, :]).astype(jnp.int32)
        for y in range(cells_y):
            index[m, pl.ds(y * near, 1), :] = left[y : y + 1]
            for x in range(cells_x):
                index[m, pl.ds(y * near + 1 + x, 1), :] = lists[m, x, pl.ds(y, 1), :]
            index[m, pl.ds(y * near + near - 1, 1), :] = right[y : y + 1]
    for y in range(cells_y):
        strip = [middle[q, y] for q in range(4)]
        centre[3, pl.ds(y * near, near), :] = strip[3][1 : 1 + near]
        strip[2] = jnp.where(strip[3] > 0.0, strip[2], far_away)
        for q in range(3):
            for move in range(3):
                table[q, move, pl.ds((y + 1) * near, near), :] = strip[q][move : move + near]
    for q in range(3):
        for move in range(3):
            for y in (0, cells_y + 1):
                table[q, move, pl.ds(y * near, near), :] = jnp.zeros((near, slots), jnp.float32)
        centre[q] = table[q, 1, pl.ds(near, centers), :]
    line = lax.broadcasted_iota(jnp.int32, (centers, slots), 0)
    for m in range(entries):
        value = index[m]
        slot, cell = value & (slots - 1), value >> shift
        picked = []
        for c in range(9):
            for q in range(3):
                source = table[q, c // 3, pl.ds((c % 3) * near, centers), :]
                got = jnp.take_along_axis(source, slot, axis=1, mode="promise_in_bounds")
                if c == 0:
                    picked.append(got)
                else:
                    picked[q] = jnp.where(cell == c, got, picked[q])
        for q in range(3):
            nearby[m, q] = picked[q]
        move_x = jnp.where(cell < 3, 0, jnp.where(cell < 6, 1, 2))
        move_y = cell - 3 * move_x
        away = ((line < near) & (move_y == 0)) | ((line >= centers - near) & (move_y == 2))
        slot_at[m] = slot
        cell_at[m] = jnp.where(away, move_x, 3)
        spots[pl.ds(m * centers, centers), :] = slot.astype(jnp.float32)
        cells[pl.ds(m * centers, centers), :] = cell.astype(jnp.float32)


def force_kernel(
    rows, centre, nearby_own, slot_at, cell_at, spots, cells, got_c, got_d, *refs,
    counts, cells_x, cells_y, capacity, turns
):
    outs = refs[: len(turns) + 1] if turns else refs[:1]
    table, parts, main, ghost = refs[len(outs) :]
    entries, centers, slots = slot_at.shape
    at_y = lax.axis_index("gy")
    even_y = lax.rem(at_y, 2) == 0
    wide, near = cells_x + 4, cells_x + 2
    has_below, has_above = at_y > 0, at_y < counts[1] - 1
    for row, swap, there in (
        (0, even_y, has_below),
        (centers - near, jnp.logical_not(even_y), has_above),
    ):
        strip = [
            jnp.where(swap, got_d[pl.ds(q * wide, wide), :], got_c[pl.ds(q * wide, wide), :])
            for q in range(4)
        ]
        full = strip[3] * there.astype(jnp.float32) > 0.0
        strip[2] = jnp.where(full, strip[2], far_away)
        for move in range(3):
            for q in range(3):
                table[q, move, pl.ds(row, near), :] = strip[q][move : move + near]
    for y in range(1, cells_y - 1):
        for move in range(3):
            for q in range(3):
                table[q, move, pl.ds(y * near, near), :] = jnp.zeros((near, slots), jnp.float32)
    center = [centre[q] for q in range(3)]
    occupied = centre[3]
    nearby = []
    for m in range(entries):
        picked = [nearby_own[m, q] for q in range(3)]
        slot, cell = slot_at[m], cell_at[m]
        for move in range(3):
            for q in range(3):
                got = jnp.take_along_axis(table[q, move], slot, axis=1, mode="promise_in_bounds")
                picked[q] = jnp.where(cell == move, got, picked[q])
        nearby.append(picked)
    grads = column_gradients(center, occupied, nearby)
    own = [sum(grads[m][q] for m in range(entries)) for q in range(3)]
    zero = jnp.zeros_like(occupied)

    def part(m, row):
        return pl.ds((m * ROWS + row) * centers, centers)

    def column_parts(m, i):
        return parts[pl.ds(m * ROWS * centers + i, ROWS, stride=centers), :]

    for m in range(entries):
        for q in range(3):
            high = grads[m][q].astype(jnp.bfloat16).astype(jnp.float32)
            parts[part(m, 3 + q), :] = high
            parts[part(m, q), :] = grads[m][q] - high
        for row in (6, 7):
            parts[part(m, row), :] = zero
    for q in range(3):
        parts[part(entries, 3 + q), :] = own[q]
    for row in (0, 1, 2, 6, 7):
        parts[part(entries, row), :] = zero
    step = 16
    ramps = [
        (lax.broadcasted_iota(jnp.int32, (step, slots), 0) + first).astype(jnp.float32).astype(jnp.bfloat16)
        for first in range(0, slots, step)
    ]
    one, none = jnp.ones((step, slots), jnp.bfloat16), jnp.zeros((step, slots), jnp.bfloat16)
    targets = [(x, y) for x in range(cells_x) for y in range(-1, cells_y + 1)]
    empty = jnp.zeros((ROWS, slots), jnp.float32)
    hot, values_at = [], []
    for y in range(cells_y):
        for x in range(-1, cells_x + 1):
            i = y * near + x + 1
            for m in range(entries):
                row = spots[pl.ds(m * centers + i, step, stride=0), :].astype(jnp.bfloat16)
                hot.append(
                    jnp.concatenate([jnp.where(ramp == row, one, none) for ramp in ramps], axis=0)
                )
                values = column_parts(m, i)
                cell = cells[pl.ds(m * centers + i, ROWS, stride=0), :]
                masked = []
                for to_x, to_y in targets:
                    dx, dy = to_x - x, to_y - y
                    near_by = -1 <= dx <= 1 and -1 <= dy <= 1
                    c = float((dx + 1) * 3 + dy + 1)
                    masked.append(jnp.where(cell == c, values, 0.0) if near_by else empty)
                values_at.append(jnp.concatenate(masked, axis=0).astype(jnp.bfloat16))
    sums = jnp.transpose(lax.dot_general(
        jnp.concatenate(hot, axis=1),
        jnp.concatenate(values_at, axis=1),
        (((1,), (1,)), ((), ())),
        preferred_element_type=jnp.float32,
    ))
    reached = {key: sums[n * ROWS : (n + 1) * ROWS] for n, key in enumerate(targets)}
    line = lax.broadcasted_iota(jnp.int32, (ROWS, slots), 0)
    kick = half_step * force_scale
    chosen = (line >= 3) & (line < 6)
    for x in range(cells_x):
        for y in range(-1, cells_y + 1):
            block = reached[x, y]
            block = block + pltpu.roll(block, 3, 0)
            if 0 <= y < cells_y:
                block = column_parts(entries, y * near + x + 1) - block
                column = rows[pl.ds((x * cells_y + y) * ROWS, ROWS), :]
                column = column + jnp.where(chosen, kick * block, 0.0)
                main[x * cells_y + y] = column
            else:
                ghost[0 if y < 0 else 1, x] = -kick * block
    places = [4 * wide + x for x in range(cells_x)]
    below = [jnp.where(even_y, got_d[pl.ds(p, 1), :], got_c[pl.ds(p, 1), :]) for p in places]
    above = [jnp.where(even_y, got_c[pl.ds(p, 1), :], got_d[pl.ds(p, 1), :]) for p in places]
    columns = [main[c] for c in range(cells_x * cells_y)]
    named_here = [
        jnp.broadcast_to(main[c, pl.ds(7, 1), :], (ROWS, slots)) for c in range(cells_x * cells_y)
    ]

    def message(owner):
        pieces = []
        for slot in range(capacity):
            wanted = (owner * capacity + slot).astype(jnp.float32)
            piece = 0.0
            for column, named in zip(columns, named_here):
                piece = piece + jnp.where(named == wanted, column, 0.0)
            pieces.append(piece[:7])
        for side, named in enumerate((below, above)):
            for slot in range(capacity):
                wanted = (owner * capacity + slot).astype(jnp.float32)
                piece = 0.0
                for x in range(cells_x):
                    piece = piece + jnp.where(named[x] == wanted, ghost[side, x, pl.ds(3, 3), :], 0.0)
                pieces.append(piece)
        return pieces

    def write(ref, pieces):
        first = 0
        for piece in pieces:
            ref[pl.ds(first, piece.shape[0]), :] = piece
            first += piece.shape[0]

    if turns:
        for ref, turn in zip(outs[:-1], turns):
            write(ref, message(round_partner(at_y, turn, counts[1])))
        write(outs[-1], message(at_y))
    else:
        for owner in range(counts[1]):
            write(outs[0].at[owner], message(jnp.int32(owner)))


def gather_kernel(*refs, count, capacity, turns):
    at_y = lax.axis_index("gy")
    if turns:
        ins, out, held = refs[:-2], refs[-2], refs[-1]
        for ref, turn in zip(ins[:-1], turns):
            held[round_partner(at_y, turn, count)] = ref[...]
        held[at_y] = ins[-1][...]
    else:
        held, out = refs
    first = capacity * 7
    for source in range(count):
        for slot in range(capacity):
            block = held[source, pl.ds(slot * 7, 7), :]
            speed = block[3:6]
            if source + 1 < count:
                speed = speed + held[source + 1, pl.ds(first + slot * 3, 3), :]
            if source > 0:
                speed = speed + held[source - 1, pl.ds(first + (capacity + slot) * 3, 3), :]
            for line in range(7):
                value = speed[line - 3 : line - 2] if 3 <= line < 6 else block[line : line + 1]
                out[source, line, pl.ds(slot, 1), :] = value


def per_device(displacement, velocity, forces, heights, counts, neighbours, plan):
    cells_x, cells_y, slots = heights.shape
    entries = neighbours.shape[0]
    sizes = (lax.axis_size("gx"), lax.axis_size("gy"))
    columns = cells_x * cells_y
    capacity = max(2, (2 * columns + sizes[1] - 1) // sizes[1])
    inputs = (displacement, velocity, forces, heights, counts, neighbours, plan.reshape(1, columns))
    whole = pl.BlockSpec(memory_space=VMEM)
    shape = lambda *dims: jax.ShapeDtypeStruct(dims, jnp.float32)
    wide, near = cells_x + 4, cells_x + 2
    centers = near * cells_y

    def swap(value, pairs):
        return lax.ppermute(value, ("gx", "gy"), pairs)

    first_size = 4 * columns + entries * cells_y
    rows, send_a, send_b = pl.pallas_call(
        functools.partial(prepare_kernel, capacity=capacity),
        out_shape=(shape(columns * ROWS, slots), shape(first_size, slots), shape(first_size, slots)),
        in_specs=[pl.BlockSpec(memory_space=HBM)] * len(inputs),
        out_specs=(whole, whole, whole),
        scratch_shapes=[pltpu.VMEM(value.shape, value.dtype) for value in inputs]
        + [pltpu.SemaphoreType.DMA((len(inputs),))],
        compiler_params=pltpu.CompilerParams(vmem_limit_bytes=VMEM_BYTES),
        name="prepare",
    )(*[pltpu.with_memory_space_constraint(value, HBM) for value in inputs])
    got_a = swap(send_a, exchange_pairs(sizes, 0, False))
    got_b = swap(send_b, exchange_pairs(sizes, 0, True))
    second_size = 4 * wide + cells_x
    middle, send_c, send_d = pl.pallas_call(
        functools.partial(strip_kernel, count_x=sizes[0], cells_x=cells_x, cells_y=cells_y),
        out_shape=(shape(4, cells_y, wide, slots), shape(second_size, slots), shape(second_size, slots)),
        in_specs=[whole] * 4,
        out_specs=(whole, whole, whole),
        compiler_params=pltpu.CompilerParams(vmem_limit_bytes=VMEM_BYTES),
        name="strips",
    )(rows, send_a, got_a, got_b)
    got_c = swap(send_c, exchange_pairs(sizes, 1, False))
    got_d = swap(send_d, exchange_pairs(sizes, 1, True))
    turns = ()
    if sizes[1] in (2, 4):
        reach = [max(abs(a - b) for a, b in round_pairs((1, sizes[1]), t)) for t in range(sizes[1] - 1)]
        turns = tuple(sorted(range(sizes[1] - 1), key=lambda turn: -reach[turn]))
    size = capacity * 13
    out_shape = (shape(size, slots),) * (len(turns) + 1) if turns else (shape(sizes[1], size, slots),)
    flat = lambda kind, *dims: jax.ShapeDtypeStruct(dims, kind)
    found = pl.pallas_call(
        functools.partial(near_kernel, cells_x=cells_x, cells_y=cells_y),
        out_shape=(
            shape(4, centers, slots),
            shape(entries, 3, centers, slots),
            flat(jnp.int32, entries, centers, slots),
            flat(jnp.int32, entries, centers, slots),
            shape(entries * centers, slots),
            shape(entries * centers, slots),
        ),
        in_specs=[whole] * 4,
        out_specs=(whole,) * 6,
        scratch_shapes=[
            pltpu.VMEM((3, 3, near * (cells_y + 2), slots), jnp.float32),
            pltpu.VMEM((entries, centers, slots), jnp.int32),
        ],
        compiler_params=pltpu.CompilerParams(vmem_limit_bytes=VMEM_BYTES),
        cost_estimate=pl.CostEstimate(flops=1000000, bytes_accessed=200000, transcendentals=0),
        name="near",
    )(middle, got_a, got_b, neighbours)
    sent = pl.pallas_call(
        functools.partial(
            force_kernel, counts=sizes, cells_x=cells_x, cells_y=cells_y, capacity=capacity, turns=turns
        ),
        out_shape=out_shape,
        in_specs=[whole] * 9,
        out_specs=tuple(whole for _ in out_shape),
        scratch_shapes=[
            pltpu.VMEM((3, 3, centers, slots), jnp.float32),
            pltpu.VMEM(((entries + 1) * ROWS * centers, slots), jnp.float32),
            pltpu.VMEM((columns, ROWS, slots), jnp.float32),
            pltpu.VMEM((2, cells_x, ROWS, slots), jnp.float32),
        ],
        compiler_params=pltpu.CompilerParams(vmem_limit_bytes=VMEM_BYTES),
        name="forces",
    )(rows, *found, got_c, got_d)
    if turns:
        arrived = [swap(value, round_pairs(sizes, turn)) for value, turn in zip(sent, turns)]
        arrived.append(sent[-1])
        scratch = [pltpu.VMEM((sizes[1], size, slots), jnp.float32)]
    else:
        arrived = [lax.all_to_all(sent[0], "gy", split_axis=0, concat_axis=0, tiled=True)]
        scratch = []
    result = pl.pallas_call(
        functools.partial(gather_kernel, count=sizes[1], capacity=capacity, turns=turns),
        out_shape=shape(sizes[1], 7, capacity, slots),
        in_specs=[whole] * len(arrived),
        out_specs=whole,
        scratch_shapes=scratch,
        compiler_params=pltpu.CompilerParams(vmem_limit_bytes=VMEM_BYTES),
        name="collect",
    )(*arrived)
    return jnp.swapaxes(result, 1, 2)[None, None]


def solution(mesh):
    in_specs = (
        P(None, "gx", "gy", None),
        P(None, "gx", "gy", None),
        P(None, "gx", "gy", None),
        P("gx", "gy", None),
        P("gx", "gy"),
        P(None, "gx", "gy", None),
        P("gx", "gy", None, None),
    )
    out_specs = P("gx", "gy", None, None, None, None)
    return jax.shard_map(
        per_device, mesh=mesh, in_specs=in_specs, out_specs=out_specs, check_vma=False
    )
```

```python
import functools

import jax
import jax.numpy as jnp
from jax import lax
from jax.experimental import pallas as pl
from jax.experimental.pallas import tpu as pltpu
from jax.sharding import PartitionSpec as P

repulse_a = 1830.8
attract_b = 471.18
decay_one = 2.4799
decay_two = 1.7322
beta_t = 1.1e-06
expo_n = 0.78734
coeff_c2 = 100390.0**2
coeff_d2 = 16.217**2
coeff_h = -0.59825
spacing = 2.4
time_step = 0.001
half_step = 0.0005
force_scale = 9648.53 / 28.0855
far_away = 1.0e6
half_pi = 1.5707963267948966
VMEM_BYTES = 8 * 2**20
ROWS = 8

VMEM = pltpu.MemorySpace.VMEM
HBM = pltpu.MemorySpace.HBM


def line_partner(place, count, odd):
    other = ((place - 1) ^ 1) + 1 if odd else place ^ 1
    return other if 0 <= other < count else None


def exchange_pairs(counts, axis, odd):
    pairs = []
    for a in range(counts[0]):
        for b in range(counts[1]):
            here = [a, b]
            other = line_partner(here[axis], counts[axis], odd)
            if other is not None:
                here[axis] = other
            else:
                spare = line_partner(here[1 - axis], counts[1 - axis], False)
                if spare is None:
                    continue
                here[1 - axis] = spare
            pairs.append((a * counts[1] + b, here[0] * counts[1] + here[1]))
    return pairs


def round_partner(place, turn, count):
    ring = count - 1
    other = lax.rem(turn - place + 2 * ring, ring)
    alone = turn * ((ring + 1) // 2) % ring
    return jnp.where(place == ring, alone, jnp.where(place == alone, ring, other))


def round_pairs(counts, turn):
    ring = counts[1] - 1
    alone = turn * ((ring + 1) // 2) % ring
    pairs = []
    for a in range(counts[0]):
        for b in range(counts[1]):
            other = alone if b == ring else ring if b == alone else (turn - b) % ring
            pairs.append((a * counts[1] + b, a * counts[1] + other))
    return pairs


def prepare_kernel(
    disp_in, vel_in, force_in, heights_in, counts_in, lists_in, plan_in,
    rows, send_a, send_b, motion, layers, counts, plan, done, *, capacity
):
    _, cells_x, cells_y, slots = disp_in.shape
    entries = lists_in.shape[0]
    for n, source in enumerate((disp_in, vel_in, force_in)):
        pltpu.make_async_copy(source, motion.at[n], done.at[0]).start()
    pltpu.make_async_copy(counts_in, counts, done.at[2]).start()
    pltpu.make_async_copy(plan_in, plan, done.at[3]).start()
    pltpu.make_async_copy(heights_in, layers.at[entries], done.at[1]).start()
    pltpu.make_async_copy(lists_in, layers.at[pl.ds(0, entries)], done.at[1]).start()
    at_x, at_y = lax.axis_index("gx"), lax.axis_index("gy")
    even_x = lax.rem(at_x, 2) == 0
    pltpu.make_async_copy(motion, motion, done.at[0]).wait()
    pltpu.make_async_copy(layers, layers, done.at[1]).wait()
    pltpu.make_async_copy(counts_in, counts, done.at[2]).wait()
    pltpu.make_async_copy(plan_in, plan, done.at[3]).wait()
    disp, vel, force = motion.at[0], motion.at[1], motion.at[2]
    heights, lists = layers.at[entries], layers
    owners = [plan[0, c] for c in range(cells_x * cells_y)]
    for x in range(cells_x):
        base_x = ((at_x * cells_x + x).astype(jnp.float32) + 0.5) * spacing
        for y in range(cells_y):
            base_y = ((at_y * cells_y + y).astype(jnp.float32) + 0.5) * spacing
            layer = heights[x, pl.ds(y, 1), :]
            occupied = (layer < counts[x, y]).astype(jnp.float32)
            lattice = (base_x, base_y, (layer.astype(jnp.float32) + 0.5) * spacing)
            column = (x * cells_y + y) * ROWS
            for q in range(3):
                pick = (q, x, pl.ds(y, 1), slice(None))
                speed = vel[pick] + half_step * (force[pick] * force_scale)
                offset = disp[pick] + time_step * speed
                rows[pl.ds(column + q, 1), :] = offset
                rows[pl.ds(column + 3 + q, 1), :] = speed
                point = lattice[q] + offset
                place = (q * cells_y + y) * cells_x + x
                send_a[pl.ds(place, 1), :] = point
                send_b[pl.ds(place, 1), :] = point
            rows[pl.ds(column + 6, 1), :] = occupied
            owner = owners[x * cells_y + y]
            earlier = sum((owners[c] == owner).astype(jnp.int32) for c in range(x * cells_y + y))
            rows[pl.ds(column + 7, 1), :] = jnp.full(
                (1, slots), jnp.asarray(owner * capacity + earlier, jnp.int32).astype(jnp.float32)
            )
            place = (3 * cells_y + y) * cells_x + x
            send_a[pl.ds(place, 1), :] = occupied
            send_b[pl.ds(place, 1), :] = occupied
    base = 4 * cells_y * cells_x
    for m in range(entries):
        low = lists[m, 0].astype(jnp.float32)
        high = lists[m, cells_x - 1].astype(jnp.float32)
        send_a[pl.ds(base + m * cells_y, cells_y), :] = jnp.where(even_x, high, low)
        send_b[pl.ds(base + m * cells_y, cells_y), :] = jnp.where(even_x, low, high)


def strip_kernel(own, got_a, got_b, middle, send_c, send_d, *, count_x, cells_x, cells_y):
    at_x, at_y = lax.axis_index("gx"), lax.axis_index("gy")
    even_x, even_y = lax.rem(at_x, 2) == 0, lax.rem(at_y, 2) == 0
    has_left = (at_x > 0).astype(jnp.float32)
    has_right = (at_x < count_x - 1).astype(jnp.float32)
    wide = cells_x + 4
    for q in range(4):
        for y in range(cells_y):
            place = (q * cells_y + y) * cells_x
            take = lambda ref: ref[pl.ds(place, cells_x), :]
            left = jnp.where(even_x, take(got_b), take(got_a))[cells_x - 2 :]
            right = jnp.where(even_x, take(got_a), take(got_b))[:2]
            if q == 3:
                left, right = left * has_left, right * has_right
            strip = jnp.concatenate([left, take(own), right], axis=0)
            middle[q, y] = strip
        low, high = middle[q, 0], middle[q, cells_y - 1]
        send_c[pl.ds(q * wide, wide), :] = jnp.where(even_y, high, low)
        send_d[pl.ds(q * wide, wide), :] = jnp.where(even_y, low, high)


def half_wave(radius):
    angle = half_pi * (jnp.clip(radius, 2.7, 3.0) - 2.85) / 0.15
    square = angle * angle
    sine, cosine = 0.0, 0.0
    for odd in (15, 13, 11, 9, 7, 5, 3, 1):
        factor_s = 1.0
        for n in range(2, odd + 1):
            factor_s /= n
        factor_c = factor_s * odd
        sign = -1.0 if odd % 4 == 3 else 1.0
        sine = sine * square + sign * factor_s
        cosine = cosine * square + sign * factor_c
    return sine * angle, cosine


def step_gate(value):
    return jnp.where(value > 1.0, 1.0, jnp.where(value == 1.0, 0.5, 0.0))


def column_gradients(center, occupied, nearby):
    entries = len(nearby)
    each = range(entries)
    inverse, gate_r, weight, slope, unit, repulse, attract = [], [], [], [], [], [], []
    for m in each:
        offset = [nearby[m][q] - center[q] for q in range(3)]
        square = offset[0] * offset[0] + offset[1] * offset[1] + offset[2] * offset[2]
        bounded = jnp.maximum(square, 1.0)
        radius = jnp.sqrt(bounded)
        inverse.append(1.0 / radius)
        gate_r.append(step_gate(square))
        sine, cosine = half_wave(radius)
        inside, outside = radius < 2.7, radius > 3.0
        weight.append(jnp.where(inside, 1.0, jnp.where(outside, 0.0, 0.5 - 0.5 * sine)))
        slope.append(jnp.where(inside | outside, 0.0, (-0.5 * half_pi / 0.15) * cosine))
        unit.append([offset[q] * inverse[m] for q in range(3)])
        repulse.append(repulse_a * jnp.exp(-decay_one * radius))
        attract.append(attract_b * jnp.exp(-decay_two * radius))
    zero = jnp.zeros_like(occupied)
    total = [zero for _ in each]
    angular, tilt = {}, {}
    for m in each:
        for k in range(m + 1, entries):
            cosine = sum(unit[m][q] * unit[k][q] for q in range(3))
            lean = coeff_h - cosine
            spread = lean * lean
            part = 1.0 / (coeff_d2 + spread)
            value = 1.0 + (coeff_c2 / coeff_d2) * (spread * part)
            angular[m, k] = value
            tilt[m, k] = (-2.0 * coeff_c2) * lean * (part * part)
            total[m] = total[m] + weight[k] * value
            total[k] = total[k] + weight[m] * value
    half = 0.5 * occupied
    pull, by_weight, by_radius = [], [], []
    for m in each:
        bond_sum = jnp.maximum(total[m], 1.0)
        power = jnp.exp(expo_n * jnp.log(beta_t * bond_sum))
        bond = jnp.exp((-0.5 / expo_n) * jnp.log(1.0 + power))
        loss = 0.5 * bond * power / ((1.0 + power) * bond_sum)
        pull.append(half * weight[m] * attract[m] * loss * step_gate(total[m]))
        by_weight.append(half * (repulse[m] - attract[m] * bond))
        by_radius.append(
            half * weight[m] * (decay_two * attract[m] * bond - decay_one * repulse[m])
        )
    by_unit = [[zero] * 3 for _ in each]
    for m in each:
        for k in range(m + 1, entries):
            by_weight[m] = by_weight[m] + pull[k] * angular[m, k]
            by_weight[k] = by_weight[k] + pull[m] * angular[m, k]
            turn = (pull[m] * weight[k] + pull[k] * weight[m]) * tilt[m, k]
            for q in range(3):
                by_unit[m][q] = by_unit[m][q] + turn * unit[k][q]
                by_unit[k][q] = by_unit[k][q] + turn * unit[m][q]
    grads = []
    for m in each:
        across = [by_unit[m][q] * inverse[m] for q in range(3)]
        along = sum(across[q] * unit[m][q] for q in range(3))
        reach = gate_r[m] * (by_radius[m] + by_weight[m] * slope[m] - along)
        grads.append([across[q] + unit[m][q] * reach for q in range(3)])
    return grads


def near_kernel(
    middle, got_a, got_b, lists, centre, nearby, slot_at, cell_at, spots, cells, table, index, *, cells_x, cells_y
):
    entries, slots = lists.shape[0], lists.shape[3]
    shift = slots.bit_length() - 1
    even_x = lax.rem(lax.axis_index("gx"), 2) == 0
    near = cells_x + 2
    centers = near * cells_y
    base = 4 * cells_x * cells_y
    for m in range(entries):
        here = pl.ds(base + m * cells_y, cells_y)
        left = jnp.where(even_x, got_b[here, :], got_a[here, :]).astype(jnp.int32)
        right = jnp.where(even_x, got_a[here, :], got_b[here, :]).astype(jnp.int32)
        for y in range(cells_y):
            index[m, pl.ds(y * near, 1), :] = left[y : y + 1]
            for x in range(cells_x):
                index[m, pl.ds(y * near + 1 + x, 1), :] = lists[m, x, pl.ds(y, 1), :]
            index[m, pl.ds(y * near + near - 1, 1), :] = right[y : y + 1]
    for y in range(cells_y):
        strip = [middle[q, y] for q in range(4)]
        centre[3, pl.ds(y * near, near), :] = strip[3][1 : 1 + near]
        strip[2] = jnp.where(strip[3] > 0.0, strip[2], far_away)
        for q in range(3):
            for move in range(3):
                table[q, move, pl.ds((y + 1) * near, near), :] = strip[q][move : move + near]
    for q in range(3):
        for move in range(3):
            for y in (0, cells_y + 1):
                table[q, move, pl.ds(y * near, near), :] = jnp.zeros((near, slots), jnp.float32)
        centre[q] = table[q, 1, pl.ds(near, centers), :]
    line = lax.broadcasted_iota(jnp.int32, (centers, slots), 0)
    for m in range(entries):
        value = index[m]
        slot, cell = value & (slots - 1), value >> shift
        picked = []
        for c in range(9):
            for q in range(3):
                source = table[q, c // 3, pl.ds((c % 3) * near, centers), :]
                got = jnp.take_along_axis(source, slot, axis=1, mode="promise_in_bounds")
                if c == 0:
                    picked.append(got)
                else:
                    picked[q] = jnp.where(cell == c, got, picked[q])
        for q in range(3):
            nearby[m, q] = picked[q]
        move_x = jnp.where(cell < 3, 0, jnp.where(cell < 6, 1, 2))
        move_y = cell - 3 * move_x
        away = ((line < near) & (move_y == 0)) | ((line >= centers - near) & (move_y == 2))
        slot_at[m] = slot
        cell_at[m] = jnp.where(away, move_x, 3)
        spots[pl.ds(m * centers, centers), :] = slot.astype(jnp.float32)
        cells[pl.ds(m * centers, centers), :] = cell.astype(jnp.float32)


def force_kernel(
    rows, centre, nearby_own, slot_at, cell_at, spots, cells, got_c, got_d, *refs,
    counts, cells_x, cells_y, capacity, turns
):
    outs = refs[: len(turns) + 1] if turns else refs[:1]
    table, parts = refs[len(outs) :]
    entries, centers, slots = slot_at.shape
    at_y = lax.axis_index("gy")
    even_y = lax.rem(at_y, 2) == 0
    wide, near = cells_x + 4, cells_x + 2
    has_below, has_above = at_y > 0, at_y < counts[1] - 1
    for row, swap, there in (
        (0, even_y, has_below),
        (centers - near, jnp.logical_not(even_y), has_above),
    ):
        strip = [
            jnp.where(swap, got_d[pl.ds(q * wide, wide), :], got_c[pl.ds(q * wide, wide), :])
            for q in range(4)
        ]
        full = strip[3] * there.astype(jnp.float32) > 0.0
        strip[2] = jnp.where(full, strip[2], far_away)
        for move in range(3):
            for q in range(3):
                table[q, move, pl.ds(row, near), :] = strip[q][move : move + near]
    for y in range(1, cells_y - 1):
        for move in range(3):
            for q in range(3):
                table[q, move, pl.ds(y * near, near), :] = jnp.zeros((near, slots), jnp.float32)
    center = [centre[q] for q in range(3)]
    occupied = centre[3]
    nearby = []
    for m in range(entries):
        picked = [nearby_own[m, q] for q in range(3)]
        slot, cell = slot_at[m], cell_at[m]
        for move in range(3):
            for q in range(3):
                got = jnp.take_along_axis(table[q, move], slot, axis=1, mode="promise_in_bounds")
                picked[q] = jnp.where(cell == move, got, picked[q])
        nearby.append(picked)
    grads = column_gradients(center, occupied, nearby)
    own = [sum(grads[m][q] for m in range(entries)) for q in range(3)]
    zero = jnp.zeros_like(occupied)

    def part(m, row):
        return pl.ds((m * ROWS + row) * centers, centers)

    def column_parts(m, i):
        return parts[pl.ds(m * ROWS * centers + i, ROWS, stride=centers), :]

    for m in range(entries):
        for q in range(3):
            high = grads[m][q].astype(jnp.bfloat16).astype(jnp.float32)
            parts[part(m, 3 + q), :] = high
            parts[part(m, q), :] = grads[m][q] - high
        for row in (6, 7):
            parts[part(m, row), :] = zero
    for q in range(3):
        parts[part(entries, 3 + q), :] = own[q]
    for row in (0, 1, 2, 6, 7):
        parts[part(entries, row), :] = zero
    step = 16
    ramps = [
        (lax.broadcasted_iota(jnp.int32, (step, slots), 0) + first).astype(jnp.float32).astype(jnp.bfloat16)
        for first in range(0, slots, step)
    ]
    one, none = jnp.ones((step, slots), jnp.bfloat16), jnp.zeros((step, slots), jnp.bfloat16)
    targets = [(x, y) for x in range(cells_x) for y in range(-1, cells_y + 1)]
    empty = jnp.zeros((ROWS, slots), jnp.float32)
    hot, values_at = [], []
    for y in range(cells_y):
        for x in range(-1, cells_x + 1):
            i = y * near + x + 1
            for m in range(entries):
                row = spots[pl.ds(m * centers + i, step, stride=0), :].astype(jnp.bfloat16)
                hot.append(
                    jnp.concatenate([jnp.where(ramp == row, one, none) for ramp in ramps], axis=0)
                )
                values = column_parts(m, i)
                cell = cells[pl.ds(m * centers + i, ROWS, stride=0), :]
                masked = []
                for to_x, to_y in targets:
                    dx, dy = to_x - x, to_y - y
                    near_by = -1 <= dx <= 1 and -1 <= dy <= 1
                    c = float((dx + 1) * 3 + dy + 1)
                    masked.append(jnp.where(cell == c, values, 0.0) if near_by else empty)
                values_at.append(jnp.concatenate(masked, axis=0).astype(jnp.bfloat16))
    sums = jnp.transpose(lax.dot_general(
        jnp.concatenate(hot, axis=1),
        jnp.concatenate(values_at, axis=1),
        (((1,), (1,)), ((), ())),
        preferred_element_type=jnp.float32,
    ))
    reached = {key: sums[n * ROWS : (n + 1) * ROWS] for n, key in enumerate(targets)}
    line = lax.broadcasted_iota(jnp.int32, (ROWS, slots), 0)
    kick = half_step * force_scale
    chosen = (line >= 3) & (line < 6)
    columns, ghosts = [], []
    for x in range(cells_x):
        for y in range(-1, cells_y + 1):
            block = reached[x, y]
            block = block + pltpu.roll(block, 3, 0)
            if 0 <= y < cells_y:
                block = column_parts(entries, y * near + x + 1) - block
                column = rows[pl.ds((x * cells_y + y) * ROWS, ROWS), :]
                column = column + jnp.where(chosen, kick * block, 0.0)
                named = jnp.broadcast_to(column[7:], (ROWS, slots))
                columns.append((named, jnp.where(line == 7, float(x * cells_y + y + 1), column)))
            else:
                ghosts.append((-kick * block)[3:6])

    def message(owner):
        pieces = []
        for slot in range(capacity):
            wanted = (owner * capacity + slot).astype(jnp.float32)
            pieces.append(sum(jnp.where(named == wanted, column, 0.0) for named, column in columns))
        return pieces + ghosts

    def write(ref, pieces):
        first = 0
        for piece in pieces:
            ref[pl.ds(first, piece.shape[0]), :] = piece
            first += piece.shape[0]

    if turns:
        for ref, turn in zip(outs[:-1], turns):
            write(ref, message(round_partner(at_y, turn, counts[1])))
        write(outs[-1], message(at_y))
    else:
        for owner in range(counts[1]):
            write(outs[0].at[owner], message(jnp.int32(owner)))


def gather_kernel(*refs, count, cells_x, cells_y, capacity, turns):
    at_y = lax.axis_index("gy")
    if turns:
        ins, out, held = refs[:-2], refs[-2], refs[-1]
        for ref, turn in zip(ins[:-1], turns):
            held[round_partner(at_y, turn, count)] = ref[...]
        held[at_y] = ins[-1][...]
    else:
        held, out = refs
    first = capacity * ROWS
    for source in range(count):
        for slot in range(capacity):
            block = held[source, pl.ds(slot * ROWS, ROWS), :]
            name = held[source, pl.ds(slot * ROWS + 7, 3, stride=0), :]
            speed = block[3:6]
            for x in range(cells_x):
                for other, y, side in ((source + 1, cells_y - 1, 0), (source - 1, 0, 1)):
                    if 0 <= other < count:
                        part = held[other, pl.ds(first + (2 * x + side) * 3, 3), :]
                        speed = speed + jnp.where(name == float(x * cells_y + y + 1), part, 0.0)
            for line in range(7):
                value = speed[line - 3 : line - 2] if 3 <= line < 6 else block[line : line + 1]
                out[source, line, pl.ds(slot, 1), :] = value


def per_device(displacement, velocity, forces, heights, counts, neighbours, plan):
    cells_x, cells_y, slots = heights.shape
    entries = neighbours.shape[0]
    sizes = (lax.axis_size("gx"), lax.axis_size("gy"))
    columns = cells_x * cells_y
    capacity = max(2, (2 * columns + sizes[1] - 1) // sizes[1])
    inputs = (displacement, velocity, forces, heights, counts, neighbours, plan.reshape(1, columns))
    whole = pl.BlockSpec(memory_space=VMEM)
    shape = lambda *dims: jax.ShapeDtypeStruct(dims, jnp.float32)
    wide, near = cells_x + 4, cells_x + 2
    centers = near * cells_y

    def swap(value, pairs):
        return lax.ppermute(value, ("gx", "gy"), pairs)

    first_size = 4 * columns + entries * cells_y
    rows, send_a, send_b = pl.pallas_call(
        functools.partial(prepare_kernel, capacity=capacity),
        out_shape=(shape(columns * ROWS, slots), shape(first_size, slots), shape(first_size, slots)),
        in_specs=[pl.BlockSpec(memory_space=HBM)] * len(inputs),
        out_specs=(whole, whole, whole),
        scratch_shapes=[
            pltpu.VMEM((3,) + displacement.shape, jnp.float32),
            pltpu.VMEM((entries + 1,) + heights.shape, jnp.int32),
            pltpu.SMEM(counts.shape, jnp.int32),
            pltpu.SMEM((1, columns), jnp.int32),
            pltpu.SemaphoreType.DMA((4,)),
        ],
        compiler_params=pltpu.CompilerParams(vmem_limit_bytes=VMEM_BYTES),
        name="prepare",
    )(*[pltpu.with_memory_space_constraint(value, HBM) for value in inputs])
    got_a = swap(send_a, exchange_pairs(sizes, 0, False))
    got_b = swap(send_b, exchange_pairs(sizes, 0, True))
    second_size = 4 * wide
    middle, send_c, send_d = pl.pallas_call(
        functools.partial(strip_kernel, count_x=sizes[0], cells_x=cells_x, cells_y=cells_y),
        out_shape=(shape(4, cells_y, wide, slots), shape(second_size, slots), shape(second_size, slots)),
        in_specs=[whole] * 3,
        out_specs=(whole, whole, whole),
        compiler_params=pltpu.CompilerParams(vmem_limit_bytes=VMEM_BYTES),
        name="strips",
    )(send_a, got_a, got_b)
    got_c = swap(send_c, exchange_pairs(sizes, 1, False))
    got_d = swap(send_d, exchange_pairs(sizes, 1, True))
    turns = ()
    if sizes[1] in (2, 4):
        reach = [max(abs(a - b) for a, b in round_pairs((1, sizes[1]), t)) for t in range(sizes[1] - 1)]
        turns = tuple(sorted(range(sizes[1] - 1), key=lambda turn: -reach[turn]))
    size = capacity * ROWS + 6 * cells_x
    out_shape = (shape(size, slots),) * (len(turns) + 1) if turns else (shape(sizes[1], size, slots),)
    flat = lambda kind, *dims: jax.ShapeDtypeStruct(dims, kind)
    found = pl.pallas_call(
        functools.partial(near_kernel, cells_x=cells_x, cells_y=cells_y),
        out_shape=(
            shape(4, centers, slots),
            shape(entries, 3, centers, slots),
            flat(jnp.int32, entries, centers, slots),
            flat(jnp.int32, entries, centers, slots),
            shape(entries * centers, slots),
            shape(entries * centers, slots),
        ),
        in_specs=[whole] * 4,
        out_specs=(whole,) * 6,
        scratch_shapes=[
            pltpu.VMEM((3, 3, near * (cells_y + 2), slots), jnp.float32),
            pltpu.VMEM((entries, centers, slots), jnp.int32),
        ],
        compiler_params=pltpu.CompilerParams(vmem_limit_bytes=VMEM_BYTES),
        cost_estimate=pl.CostEstimate(flops=1000000, bytes_accessed=200000, transcendentals=0),
        name="near",
    )(middle, got_a, got_b, neighbours)
    sent = pl.pallas_call(
        functools.partial(
            force_kernel, counts=sizes, cells_x=cells_x, cells_y=cells_y, capacity=capacity, turns=turns
        ),
        out_shape=out_shape,
        in_specs=[whole] * 9,
        out_specs=tuple(whole for _ in out_shape),
        scratch_shapes=[
            pltpu.VMEM((3, 3, centers, slots), jnp.float32),
            pltpu.VMEM(((entries + 1) * ROWS * centers, slots), jnp.float32),
        ],
        compiler_params=pltpu.CompilerParams(vmem_limit_bytes=VMEM_BYTES),
        name="forces",
    )(rows, *found, got_c, got_d)
    if turns:
        arrived = [swap(value, round_pairs(sizes, turn)) for value, turn in zip(sent, turns)]
        arrived.append(sent[-1])
        scratch = [pltpu.VMEM((sizes[1], size, slots), jnp.float32)]
    else:
        arrived = [lax.all_to_all(sent[0], "gy", split_axis=0, concat_axis=0, tiled=True)]
        scratch = []
    result = pl.pallas_call(
        functools.partial(
            gather_kernel, count=sizes[1], cells_x=cells_x, cells_y=cells_y, capacity=capacity, turns=turns
        ),
        out_shape=shape(sizes[1], 7, capacity, slots),
        in_specs=[whole] * len(arrived),
        out_specs=whole,
        scratch_shapes=scratch,
        compiler_params=pltpu.CompilerParams(vmem_limit_bytes=VMEM_BYTES),
        name="collect",
    )(*arrived)
    return jnp.swapaxes(result, 1, 2)[None, None]


def solution(mesh):
    in_specs = (
        P(None, "gx", "gy", None),
        P(None, "gx", "gy", None),
        P(None, "gx", "gy", None),
        P("gx", "gy", None),
        P("gx", "gy"),
        P(None, "gx", "gy", None),
        P("gx", "gy", None, None),
    )
    out_specs = P("gx", "gy", None, None, None, None)
    return jax.shard_map(
        per_device, mesh=mesh, in_specs=in_specs, out_specs=out_specs, check_vma=False
    )
```

```python
import functools

import jax
import jax.numpy as jnp
from jax import lax
from jax.experimental import pallas as pl
from jax.experimental.pallas import tpu as pltpu
from jax.sharding import PartitionSpec as P

repulse_a = 1830.8
attract_b = 471.18
decay_one = 2.4799
decay_two = 1.7322
beta_t = 1.1e-06
expo_n = 0.78734
coeff_c2 = 100390.0**2
coeff_d2 = 16.217**2
coeff_h = -0.59825
spacing = 2.4
time_step = 0.001
half_step = 0.0005
force_scale = 9648.53 / 28.0855
far_away = 1.0e6
half_pi = 1.5707963267948966
VMEM_BYTES = 8 * 2**20
ROWS = 8

VMEM = pltpu.MemorySpace.VMEM
HBM = pltpu.MemorySpace.HBM


def line_partner(place, count, odd):
    other = ((place - 1) ^ 1) + 1 if odd else place ^ 1
    return other if 0 <= other < count else None


def exchange_pairs(counts, axis, odd):
    pairs = []
    for a in range(counts[0]):
        for b in range(counts[1]):
            here = [a, b]
            other = line_partner(here[axis], counts[axis], odd)
            if other is not None:
                here[axis] = other
            else:
                spare = line_partner(here[1 - axis], counts[1 - axis], False)
                if spare is None:
                    continue
                here[1 - axis] = spare
            pairs.append((a * counts[1] + b, here[0] * counts[1] + here[1]))
    return pairs


def circle_pairs(counts, rising):
    pairs = []
    for a in range(counts[0]):
        for b in range(counts[1]):
            other = (a, b + (1 if a % 2 == rising else -1))
            if not 0 <= other[1] < counts[1]:
                other = (a ^ 1, b)
            if other[0] < counts[0]:
                pairs.append((a * counts[1] + b, other[0] * counts[1] + other[1]))
    return pairs


def rounds(count):
    if count == 4:
        circuit = (0, 2, 1, 3)
        ahead, back = [
            tuple(circuit[(circuit.index(place) + way) % count] for place in range(count))
            for way in (1, -1)
        ]
        return (ahead, back, tuple(place ^ 1 for place in range(count)))
    return ((1, 0),) if count == 2 else ()


def named_by(table, place):
    return sum(jnp.where(place == n, other, 0) for n, other in enumerate(table))


def prepare_kernel(
    disp_in, vel_in, force_in, heights_in, counts_in, lists_in, plan_in,
    rows, send_a, send_b, motion, layers, counts, plan, done, *, capacity
):
    _, cells_x, cells_y, slots = disp_in.shape
    entries = lists_in.shape[0]
    for n, source in enumerate((disp_in, vel_in, force_in)):
        pltpu.make_async_copy(source, motion.at[n], done.at[0]).start()
    pltpu.make_async_copy(counts_in, counts, done.at[2]).start()
    pltpu.make_async_copy(plan_in, plan, done.at[3]).start()
    pltpu.make_async_copy(heights_in, layers.at[entries], done.at[1]).start()
    pltpu.make_async_copy(lists_in, layers.at[pl.ds(0, entries)], done.at[1]).start()
    at_x, at_y = lax.axis_index("gx"), lax.axis_index("gy")
    even_x = lax.rem(at_x, 2) == 0
    pltpu.make_async_copy(motion, motion, done.at[0]).wait()
    pltpu.make_async_copy(layers, layers, done.at[1]).wait()
    pltpu.make_async_copy(counts_in, counts, done.at[2]).wait()
    pltpu.make_async_copy(plan_in, plan, done.at[3]).wait()
    disp, vel, force = motion.at[0], motion.at[1], motion.at[2]
    heights, lists = layers.at[entries], layers
    owners = [plan[0, c] for c in range(cells_x * cells_y)]
    for x in range(cells_x):
        base_x = ((at_x * cells_x + x).astype(jnp.float32) + 0.5) * spacing
        for y in range(cells_y):
            base_y = ((at_y * cells_y + y).astype(jnp.float32) + 0.5) * spacing
            layer = heights[x, pl.ds(y, 1), :]
            occupied = (layer < counts[x, y]).astype(jnp.float32)
            lattice = (base_x, base_y, (layer.astype(jnp.float32) + 0.5) * spacing)
            column = (x * cells_y + y) * ROWS
            for q in range(3):
                pick = (q, x, pl.ds(y, 1), slice(None))
                speed = vel[pick] + half_step * (force[pick] * force_scale)
                offset = disp[pick] + time_step * speed
                rows[pl.ds(column + q, 1), :] = offset
                rows[pl.ds(column + 3 + q, 1), :] = speed
                point = lattice[q] + offset
                place = (q * cells_y + y) * cells_x + x
                send_a[pl.ds(place, 1), :] = point
                send_b[pl.ds(place, 1), :] = point
            rows[pl.ds(column + 6, 1), :] = occupied
            owner = owners[x * cells_y + y]
            earlier = sum((owners[c] == owner).astype(jnp.int32) for c in range(x * cells_y + y))
            rows[pl.ds(column + 7, 1), :] = jnp.full(
                (1, slots), jnp.asarray(owner * capacity + earlier, jnp.int32).astype(jnp.float32)
            )
            place = (3 * cells_y + y) * cells_x + x
            send_a[pl.ds(place, 1), :] = occupied
            send_b[pl.ds(place, 1), :] = occupied
    base = 4 * cells_y * cells_x
    for m in range(entries):
        low = lists[m, 0].astype(jnp.float32)
        high = lists[m, cells_x - 1].astype(jnp.float32)
        send_a[pl.ds(base + m * cells_y, cells_y), :] = jnp.where(even_x, high, low)
        send_b[pl.ds(base + m * cells_y, cells_y), :] = jnp.where(even_x, low, high)


def strip_kernel(own, got_a, got_b, middle, send_c, send_d, *, count_x, cells_x, cells_y):
    at_x = lax.axis_index("gx")
    even_x = lax.rem(at_x, 2) == 0
    has_left = (at_x > 0).astype(jnp.float32)
    has_right = (at_x < count_x - 1).astype(jnp.float32)
    wide = cells_x + 4
    for q in range(4):
        for y in range(cells_y):
            place = (q * cells_y + y) * cells_x
            take = lambda ref: ref[pl.ds(place, cells_x), :]
            left = jnp.where(even_x, take(got_b), take(got_a))[cells_x - 2 :]
            right = jnp.where(even_x, take(got_a), take(got_b))[:2]
            if q == 3:
                left, right = left * has_left, right * has_right
            strip = jnp.concatenate([left, take(own), right], axis=0)
            middle[q, y] = strip
        low, high = middle[q, 0], middle[q, cells_y - 1]
        send_c[pl.ds(q * wide, wide), :] = jnp.where(even_x, low, high)
        send_d[pl.ds(q * wide, wide), :] = jnp.where(even_x, high, low)


def half_wave(radius):
    angle = half_pi * (jnp.clip(radius, 2.7, 3.0) - 2.85) / 0.15
    square = angle * angle
    sine, cosine = 0.0, 0.0
    for odd in (15, 13, 11, 9, 7, 5, 3, 1):
        factor_s = 1.0
        for n in range(2, odd + 1):
            factor_s /= n
        factor_c = factor_s * odd
        sign = -1.0 if odd % 4 == 3 else 1.0
        sine = sine * square + sign * factor_s
        cosine = cosine * square + sign * factor_c
    return sine * angle, cosine


def step_gate(value):
    return jnp.where(value > 1.0, 1.0, jnp.where(value == 1.0, 0.5, 0.0))


def column_gradients(center, occupied, nearby):
    entries = len(nearby)
    each = range(entries)
    inverse, gate_r, weight, slope, unit, repulse, attract = [], [], [], [], [], [], []
    for m in each:
        offset = [nearby[m][q] - center[q] for q in range(3)]
        square = offset[0] * offset[0] + offset[1] * offset[1] + offset[2] * offset[2]
        bounded = jnp.maximum(square, 1.0)
        radius = jnp.sqrt(bounded)
        inverse.append(1.0 / radius)
        gate_r.append(step_gate(square))
        sine, cosine = half_wave(radius)
        inside, outside = radius < 2.7, radius > 3.0
        weight.append(jnp.where(inside, 1.0, jnp.where(outside, 0.0, 0.5 - 0.5 * sine)))
        slope.append(jnp.where(inside | outside, 0.0, (-0.5 * half_pi / 0.15) * cosine))
        unit.append([offset[q] * inverse[m] for q in range(3)])
        repulse.append(repulse_a * jnp.exp(-decay_one * radius))
        attract.append(attract_b * jnp.exp(-decay_two * radius))
    zero = jnp.zeros_like(occupied)
    total = [zero for _ in each]
    angular, tilt = {}, {}
    for m in each:
        for k in range(m + 1, entries):
            cosine = sum(unit[m][q] * unit[k][q] for q in range(3))
            lean = coeff_h - cosine
            spread = lean * lean
            part = 1.0 / (coeff_d2 + spread)
            value = 1.0 + (coeff_c2 / coeff_d2) * (spread * part)
            angular[m, k] = value
            tilt[m, k] = (-2.0 * coeff_c2) * lean * (part * part)
            total[m] = total[m] + weight[k] * value
            total[k] = total[k] + weight[m] * value
    half = 0.5 * occupied
    pull, by_weight, by_radius = [], [], []
    for m in each:
        bond_sum = jnp.maximum(total[m], 1.0)
        power = jnp.exp(expo_n * jnp.log(beta_t * bond_sum))
        bond = jnp.exp((-0.5 / expo_n) * jnp.log(1.0 + power))
        loss = 0.5 * bond * power / ((1.0 + power) * bond_sum)
        pull.append(half * weight[m] * attract[m] * loss * step_gate(total[m]))
        by_weight.append(half * (repulse[m] - attract[m] * bond))
        by_radius.append(
            half * weight[m] * (decay_two * attract[m] * bond - decay_one * repulse[m])
        )
    by_unit = [[zero] * 3 for _ in each]
    for m in each:
        for k in range(m + 1, entries):
            by_weight[m] = by_weight[m] + pull[k] * angular[m, k]
            by_weight[k] = by_weight[k] + pull[m] * angular[m, k]
            turn = (pull[m] * weight[k] + pull[k] * weight[m]) * tilt[m, k]
            for q in range(3):
                by_unit[m][q] = by_unit[m][q] + turn * unit[k][q]
                by_unit[k][q] = by_unit[k][q] + turn * unit[m][q]
    grads = []
    for m in each:
        across = [by_unit[m][q] * inverse[m] for q in range(3)]
        along = sum(across[q] * unit[m][q] for q in range(3))
        reach = gate_r[m] * (by_radius[m] + by_weight[m] * slope[m] - along)
        grads.append([across[q] + unit[m][q] * reach for q in range(3)])
    return grads


def near_kernel(
    middle, got_a, got_b, lists, centre, nearby, slot_at, cell_at, spots, cells, table, index, *, cells_x, cells_y
):
    entries, slots = lists.shape[0], lists.shape[3]
    shift = slots.bit_length() - 1
    even_x = lax.rem(lax.axis_index("gx"), 2) == 0
    near = cells_x + 2
    centers = near * cells_y
    base = 4 * cells_x * cells_y
    for m in range(entries):
        here = pl.ds(base + m * cells_y, cells_y)
        left = jnp.where(even_x, got_b[here, :], got_a[here, :]).astype(jnp.int32)
        right = jnp.where(even_x, got_a[here, :], got_b[here, :]).astype(jnp.int32)
        for y in range(cells_y):
            index[m, pl.ds(y * near, 1), :] = left[y : y + 1]
            for x in range(cells_x):
                index[m, pl.ds(y * near + 1 + x, 1), :] = lists[m, x, pl.ds(y, 1), :]
            index[m, pl.ds(y * near + near - 1, 1), :] = right[y : y + 1]
    for y in range(cells_y):
        strip = [middle[q, y] for q in range(4)]
        centre[3, pl.ds(y * near, near), :] = strip[3][1 : 1 + near]
        strip[2] = jnp.where(strip[3] > 0.0, strip[2], far_away)
        for q in range(3):
            for move in range(3):
                table[q, move, pl.ds((y + 1) * near, near), :] = strip[q][move : move + near]
    for q in range(3):
        for move in range(3):
            for y in (0, cells_y + 1):
                table[q, move, pl.ds(y * near, near), :] = jnp.zeros((near, slots), jnp.float32)
        centre[q] = table[q, 1, pl.ds(near, centers), :]
    line = lax.broadcasted_iota(jnp.int32, (centers, slots), 0)
    for m in range(entries):
        value = index[m]
        slot, cell = value & (slots - 1), value >> shift
        picked = []
        for c in range(9):
            for q in range(3):
                source = table[q, c // 3, pl.ds((c % 3) * near, centers), :]
                got = jnp.take_along_axis(source, slot, axis=1, mode="promise_in_bounds")
                if c == 0:
                    picked.append(got)
                else:
                    picked[q] = jnp.where(cell == c, got, picked[q])
        for q in range(3):
            nearby[m, q] = picked[q]
        move_x = jnp.where(cell < 3, 0, jnp.where(cell < 6, 1, 2))
        move_y = cell - 3 * move_x
        away = ((line < near) & (move_y == 0)) | ((line >= centers - near) & (move_y == 2))
        slot_at[m] = slot
        cell_at[m] = jnp.where(away, move_x, 3)
        spots[pl.ds(m * centers, centers), :] = slot.astype(jnp.float32)
        cells[pl.ds(m * centers, centers), :] = cell.astype(jnp.float32)


def force_kernel(
    rows, centre, nearby_own, slot_at, cell_at, spots, cells, got_c, got_d, *refs,
    counts, cells_x, cells_y, capacity, turns
):
    outs = refs[: len(turns) + 1] if turns else refs[:1]
    table, parts = refs[len(outs) :]
    entries, centers, slots = slot_at.shape
    at_y = lax.axis_index("gy")
    even_x = lax.rem(lax.axis_index("gx"), 2) == 0
    wide, near = cells_x + 4, cells_x + 2
    has_below, has_above = at_y > 0, at_y < counts[1] - 1
    for row, swap, there in (
        (0, even_x, has_below),
        (centers - near, jnp.logical_not(even_x), has_above),
    ):
        strip = [
            jnp.where(swap, got_d[pl.ds(q * wide, wide), :], got_c[pl.ds(q * wide, wide), :])
            for q in range(4)
        ]
        full = strip[3] * there.astype(jnp.float32) > 0.0
        strip[2] = jnp.where(full, strip[2], far_away)
        for move in range(3):
            for q in range(3):
                table[q, move, pl.ds(row, near), :] = strip[q][move : move + near]
    for y in range(1, cells_y - 1):
        for move in range(3):
            for q in range(3):
                table[q, move, pl.ds(y * near, near), :] = jnp.zeros((near, slots), jnp.float32)
    center = [centre[q] for q in range(3)]
    occupied = centre[3]
    nearby = []
    for m in range(entries):
        picked = [nearby_own[m, q] for q in range(3)]
        slot, cell = slot_at[m], cell_at[m]
        for move in range(3):
            for q in range(3):
                got = jnp.take_along_axis(table[q, move], slot, axis=1, mode="promise_in_bounds")
                picked[q] = jnp.where(cell == move, got, picked[q])
        nearby.append(picked)
    grads = column_gradients(center, occupied, nearby)
    own = [sum(grads[m][q] for m in range(entries)) for q in range(3)]
    zero = jnp.zeros_like(occupied)

    def part(m, row):
        return pl.ds((m * ROWS + row) * centers, centers)

    def column_parts(m, i):
        return parts[pl.ds(m * ROWS * centers + i, ROWS, stride=centers), :]

    for m in range(entries):
        for q in range(3):
            high = grads[m][q].astype(jnp.bfloat16).astype(jnp.float32)
            parts[part(m, 3 + q), :] = high
            parts[part(m, q), :] = grads[m][q] - high
        for row in (6, 7):
            parts[part(m, row), :] = zero
    for q in range(3):
        parts[part(entries, 3 + q), :] = own[q]
    for row in (0, 1, 2, 6, 7):
        parts[part(entries, row), :] = zero
    step = 16
    ramps = [
        (lax.broadcasted_iota(jnp.int32, (step, slots), 0) + first).astype(jnp.float32).astype(jnp.bfloat16)
        for first in range(0, slots, step)
    ]
    one, none = jnp.ones((step, slots), jnp.bfloat16), jnp.zeros((step, slots), jnp.bfloat16)
    targets = [(x, y) for x in range(cells_x) for y in range(-1, cells_y + 1)]
    empty = jnp.zeros((ROWS, slots), jnp.float32)
    hot, values_at = [], []
    for y in range(cells_y):
        for x in range(-1, cells_x + 1):
            i = y * near + x + 1
            for m in range(entries):
                row = spots[pl.ds(m * centers + i, step, stride=0), :].astype(jnp.bfloat16)
                hot.append(
                    jnp.concatenate([jnp.where(ramp == row, one, none) for ramp in ramps], axis=0)
                )
                values = column_parts(m, i)
                cell = cells[pl.ds(m * centers + i, ROWS, stride=0), :]
                masked = []
                for to_x, to_y in targets:
                    dx, dy = to_x - x, to_y - y
                    near_by = -1 <= dx <= 1 and -1 <= dy <= 1
                    c = float((dx + 1) * 3 + dy + 1)
                    masked.append(jnp.where(cell == c, values, 0.0) if near_by else empty)
                values_at.append(jnp.concatenate(masked, axis=0).astype(jnp.bfloat16))
    sums = jnp.transpose(lax.dot_general(
        jnp.concatenate(hot, axis=1),
        jnp.concatenate(values_at, axis=1),
        (((1,), (1,)), ((), ())),
        preferred_element_type=jnp.float32,
    ))
    reached = {key: sums[n * ROWS : (n + 1) * ROWS] for n, key in enumerate(targets)}
    line = lax.broadcasted_iota(jnp.int32, (ROWS, slots), 0)
    kick = half_step * force_scale
    chosen = (line >= 3) & (line < 6)
    columns, ghosts = [], []
    for x in range(cells_x):
        for y in range(-1, cells_y + 1):
            block = reached[x, y]
            block = block + pltpu.roll(block, 3, 0)
            if 0 <= y < cells_y:
                block = column_parts(entries, y * near + x + 1) - block
                column = rows[pl.ds((x * cells_y + y) * ROWS, ROWS), :]
                column = column + jnp.where(chosen, kick * block, 0.0)
                named = jnp.broadcast_to(column[7:], (ROWS, slots))
                columns.append((named, jnp.where(line == 7, float(x * cells_y + y + 1), column)))
            else:
                ghosts.append((-kick * block)[3:6])

    def message(owner):
        pieces = []
        for slot in range(capacity):
            wanted = (owner * capacity + slot).astype(jnp.float32)
            pieces.append(sum(jnp.where(named == wanted, column, 0.0) for named, column in columns))
        return pieces + ghosts

    def write(ref, pieces):
        first = 0
        for piece in pieces:
            ref[pl.ds(first, piece.shape[0]), :] = piece
            first += piece.shape[0]

    if turns:
        for ref, turn in zip(outs[:-1], turns):
            write(ref, message(named_by(turn, at_y)))
        write(outs[-1], message(at_y))
    else:
        for owner in range(counts[1]):
            write(outs[0].at[owner], message(jnp.int32(owner)))


def gather_kernel(*refs, count, cells_x, cells_y, capacity, turns):
    at_y = lax.axis_index("gy")
    if turns:
        ins, out, held = refs[:-2], refs[-2], refs[-1]
        for ref, turn in zip(ins[:-1], turns):
            held[named_by([turn.index(n) for n in range(count)], at_y)] = ref[...]
        held[at_y] = ins[-1][...]
    else:
        held, out = refs
    first = capacity * ROWS
    for source in range(count):
        for slot in range(capacity):
            block = held[source, pl.ds(slot * ROWS, ROWS), :]
            name = held[source, pl.ds(slot * ROWS + 7, 3, stride=0), :]
            speed = block[3:6]
            for x in range(cells_x):
                for other, y, side in ((source + 1, cells_y - 1, 0), (source - 1, 0, 1)):
                    if 0 <= other < count:
                        part = held[other, pl.ds(first + (2 * x + side) * 3, 3), :]
                        speed = speed + jnp.where(name == float(x * cells_y + y + 1), part, 0.0)
            for line in range(7):
                value = speed[line - 3 : line - 2] if 3 <= line < 6 else block[line : line + 1]
                out[source, line, pl.ds(slot, 1), :] = value


def per_device(displacement, velocity, forces, heights, counts, neighbours, plan):
    cells_x, cells_y, slots = heights.shape
    entries = neighbours.shape[0]
    sizes = (lax.axis_size("gx"), lax.axis_size("gy"))
    columns = cells_x * cells_y
    capacity = max(2, (2 * columns + sizes[1] - 1) // sizes[1])
    inputs = (displacement, velocity, forces, heights, counts, neighbours, plan.reshape(1, columns))
    whole = pl.BlockSpec(memory_space=VMEM)
    shape = lambda *dims: jax.ShapeDtypeStruct(dims, jnp.float32)
    wide, near = cells_x + 4, cells_x + 2
    centers = near * cells_y

    def swap(value, pairs):
        return lax.ppermute(value, ("gx", "gy"), pairs)

    first_size = 4 * columns + entries * cells_y
    rows, send_a, send_b = pl.pallas_call(
        functools.partial(prepare_kernel, capacity=capacity),
        out_shape=(shape(columns * ROWS, slots), shape(first_size, slots), shape(first_size, slots)),
        in_specs=[pl.BlockSpec(memory_space=HBM)] * len(inputs),
        out_specs=(whole, whole, whole),
        scratch_shapes=[
            pltpu.VMEM((3,) + displacement.shape, jnp.float32),
            pltpu.VMEM((entries + 1,) + heights.shape, jnp.int32),
            pltpu.SMEM(counts.shape, jnp.int32),
            pltpu.SMEM((1, columns), jnp.int32),
            pltpu.SemaphoreType.DMA((4,)),
        ],
        compiler_params=pltpu.CompilerParams(vmem_limit_bytes=VMEM_BYTES),
        name="prepare",
    )(*[pltpu.with_memory_space_constraint(value, HBM) for value in inputs])
    got_a = swap(send_a, exchange_pairs(sizes, 0, False))
    got_b = swap(send_b, exchange_pairs(sizes, 0, True))
    second_size = 4 * wide
    middle, send_c, send_d = pl.pallas_call(
        functools.partial(strip_kernel, count_x=sizes[0], cells_x=cells_x, cells_y=cells_y),
        out_shape=(shape(4, cells_y, wide, slots), shape(second_size, slots), shape(second_size, slots)),
        in_specs=[whole] * 3,
        out_specs=(whole, whole, whole),
        compiler_params=pltpu.CompilerParams(vmem_limit_bytes=VMEM_BYTES),
        name="strips",
    )(send_a, got_a, got_b)
    got_c = swap(send_c, circle_pairs(sizes, 1))
    got_d = swap(send_d, circle_pairs(sizes, 0))
    turns = rounds(sizes[1])
    size = capacity * ROWS + 6 * cells_x
    out_shape = (shape(size, slots),) * (len(turns) + 1) if turns else (shape(sizes[1], size, slots),)
    flat = lambda kind, *dims: jax.ShapeDtypeStruct(dims, kind)
    found = pl.pallas_call(
        functools.partial(near_kernel, cells_x=cells_x, cells_y=cells_y),
        out_shape=(
            shape(4, centers, slots),
            shape(entries, 3, centers, slots),
            flat(jnp.int32, entries, centers, slots),
            flat(jnp.int32, entries, centers, slots),
            shape(entries * centers, slots),
            shape(entries * centers, slots),
        ),
        in_specs=[whole] * 4,
        out_specs=(whole,) * 6,
        scratch_shapes=[
            pltpu.VMEM((3, 3, near * (cells_y + 2), slots), jnp.float32),
            pltpu.VMEM((entries, centers, slots), jnp.int32),
        ],
        compiler_params=pltpu.CompilerParams(vmem_limit_bytes=VMEM_BYTES),
        cost_estimate=pl.CostEstimate(flops=1000000, bytes_accessed=200000, transcendentals=0),
        name="near",
    )(middle, got_a, got_b, neighbours)
    sent = pl.pallas_call(
        functools.partial(
            force_kernel, counts=sizes, cells_x=cells_x, cells_y=cells_y, capacity=capacity, turns=turns
        ),
        out_shape=out_shape,
        in_specs=[whole] * 9,
        out_specs=tuple(whole for _ in out_shape),
        scratch_shapes=[
            pltpu.VMEM((3, 3, centers, slots), jnp.float32),
            pltpu.VMEM(((entries + 1) * ROWS * centers, slots), jnp.float32),
        ],
        compiler_params=pltpu.CompilerParams(vmem_limit_bytes=VMEM_BYTES),
        name="forces",
    )(rows, *found, got_c, got_d)
    if turns:
        arrived = [lax.ppermute(value, "gy", list(enumerate(turn))) for value, turn in zip(sent, turns)]
        arrived.append(sent[-1])
        scratch = [pltpu.VMEM((sizes[1], size, slots), jnp.float32)]
    else:
        arrived = [lax.all_to_all(sent[0], "gy", split_axis=0, concat_axis=0, tiled=True)]
        scratch = []
    result = pl.pallas_call(
        functools.partial(
            gather_kernel, count=sizes[1], cells_x=cells_x, cells_y=cells_y, capacity=capacity, turns=turns
        ),
        out_shape=shape(sizes[1], 7, capacity, slots),
        in_specs=[whole] * len(arrived),
        out_specs=whole,
        scratch_shapes=scratch,
        compiler_params=pltpu.CompilerParams(vmem_limit_bytes=VMEM_BYTES),
        name="collect",
    )(*arrived)
    return jnp.swapaxes(result, 1, 2)[None, None]


def solution(mesh):
    in_specs = (
        P(None, "gx", "gy", None),
        P(None, "gx", "gy", None),
        P(None, "gx", "gy", None),
        P("gx", "gy", None),
        P("gx", "gy"),
        P(None, "gx", "gy", None),
        P("gx", "gy", None, None),
    )
    out_specs = P("gx", "gy", None, None, None, None)
    return jax.shard_map(
        per_device, mesh=mesh, in_specs=in_specs, out_specs=out_specs, check_vma=False
    )
```

```python
import functools

import jax
import jax.numpy as jnp
from jax import lax
from jax.experimental import pallas as pl
from jax.experimental.pallas import tpu as pltpu
from jax.sharding import PartitionSpec as P

repulse_a = 1830.8
attract_b = 471.18
decay_one = 2.4799
decay_two = 1.7322
beta_t = 1.1e-06
expo_n = 0.78734
coeff_c2 = 100390.0**2
coeff_d2 = 16.217**2
coeff_h = -0.59825
spacing = 2.4
time_step = 0.001
half_step = 0.0005
force_scale = 9648.53 / 28.0855
far_away = 1.0e6
half_pi = 1.5707963267948966
VMEM_BYTES = 8 * 2**20
ROWS = 8

VMEM = pltpu.MemorySpace.VMEM
HBM = pltpu.MemorySpace.HBM


def line_partner(place, count, odd):
    other = ((place - 1) ^ 1) + 1 if odd else place ^ 1
    return other if 0 <= other < count else None


def exchange_pairs(counts, axis, odd):
    pairs = []
    for a in range(counts[0]):
        for b in range(counts[1]):
            here = [a, b]
            other = line_partner(here[axis], counts[axis], odd)
            if other is not None:
                here[axis] = other
            else:
                spare = line_partner(here[1 - axis], counts[1 - axis], False)
                if spare is None:
                    continue
                here[1 - axis] = spare
            pairs.append((a * counts[1] + b, here[0] * counts[1] + here[1]))
    return pairs


def circle_pairs(counts, rising):
    pairs = []
    for a in range(counts[0]):
        for b in range(counts[1]):
            other = (a, b + (1 if a % 2 == rising else -1))
            if not 0 <= other[1] < counts[1]:
                other = (a ^ 1, b)
            if other[0] < counts[0]:
                pairs.append((a * counts[1] + b, other[0] * counts[1] + other[1]))
    return pairs


def rounds(count):
    if count == 4:
        circuit = (0, 2, 1, 3)
        ahead, back = [
            tuple(circuit[(circuit.index(place) + way) % count] for place in range(count))
            for way in (1, -1)
        ]
        return (ahead, back, tuple(place ^ 1 for place in range(count)))
    return ((1, 0),) if count == 2 else ()


def named_by(table, place):
    return sum(jnp.where(place == n, other, 0) for n, other in enumerate(table))


def prepare_kernel(
    disp_in, vel_in, force_in, heights_in, counts_in, lists_in, plan_in,
    rows, send_a, send_b, motion, layers, counts, plan, done, *, capacity
):
    _, cells_x, cells_y, slots = disp_in.shape
    entries = lists_in.shape[0]
    for n, source in enumerate((disp_in, vel_in, force_in)):
        pltpu.make_async_copy(source, motion.at[n], done.at[0]).start()
    pltpu.make_async_copy(counts_in, counts, done.at[2]).start()
    pltpu.make_async_copy(plan_in, plan, done.at[3]).start()
    pltpu.make_async_copy(heights_in, layers.at[entries], done.at[1]).start()
    pltpu.make_async_copy(lists_in, layers.at[pl.ds(0, entries)], done.at[1]).start()
    at_x, at_y = lax.axis_index("gx"), lax.axis_index("gy")
    even_x = lax.rem(at_x, 2) == 0
    pltpu.make_async_copy(motion, motion, done.at[0]).wait()
    pltpu.make_async_copy(layers, layers, done.at[1]).wait()
    pltpu.make_async_copy(counts_in, counts, done.at[2]).wait()
    pltpu.make_async_copy(plan_in, plan, done.at[3]).wait()
    disp, vel, force = motion.at[0], motion.at[1], motion.at[2]
    heights, lists = layers.at[entries], layers
    owners = [plan[0, c] for c in range(cells_x * cells_y)]
    for x in range(cells_x):
        base_x = ((at_x * cells_x + x).astype(jnp.float32) + 0.5) * spacing
        for y in range(cells_y):
            base_y = ((at_y * cells_y + y).astype(jnp.float32) + 0.5) * spacing
            layer = heights[x, pl.ds(y, 1), :]
            occupied = (layer < counts[x, y]).astype(jnp.float32)
            lattice = (base_x, base_y, (layer.astype(jnp.float32) + 0.5) * spacing)
            column = (x * cells_y + y) * ROWS
            for q in range(3):
                pick = (q, x, pl.ds(y, 1), slice(None))
                speed = vel[pick] + half_step * (force[pick] * force_scale)
                offset = disp[pick] + time_step * speed
                rows[pl.ds(column + q, 1), :] = offset
                rows[pl.ds(column + 3 + q, 1), :] = speed
                point = lattice[q] + offset
                place = (q * cells_y + y) * cells_x + x
                send_a[pl.ds(place, 1), :] = point
                send_b[pl.ds(place, 1), :] = point
            rows[pl.ds(column + 6, 1), :] = occupied
            owner = owners[x * cells_y + y]
            earlier = sum((owners[c] == owner).astype(jnp.int32) for c in range(x * cells_y + y))
            rows[pl.ds(column + 7, 1), :] = jnp.full(
                (1, slots), jnp.asarray(owner * capacity + earlier, jnp.int32).astype(jnp.float32)
            )
            place = (3 * cells_y + y) * cells_x + x
            send_a[pl.ds(place, 1), :] = occupied
            send_b[pl.ds(place, 1), :] = occupied
    base = 4 * cells_y * cells_x
    for m in range(entries):
        low = lists[m, 0].astype(jnp.float32)
        high = lists[m, cells_x - 1].astype(jnp.float32)
        send_a[pl.ds(base + m * cells_y, cells_y), :] = jnp.where(even_x, high, low)
        send_b[pl.ds(base + m * cells_y, cells_y), :] = jnp.where(even_x, low, high)


def strip_kernel(own, got_a, got_b, middle, send_c, send_d, *, count_x, cells_x, cells_y):
    at_x = lax.axis_index("gx")
    even_x = lax.rem(at_x, 2) == 0
    has_left = (at_x > 0).astype(jnp.float32)
    has_right = (at_x < count_x - 1).astype(jnp.float32)
    wide = cells_x + 4
    for q in range(4):
        for y in range(cells_y):
            place = (q * cells_y + y) * cells_x
            take = lambda ref: ref[pl.ds(place, cells_x), :]
            left = jnp.where(even_x, take(got_b), take(got_a))[cells_x - 2 :]
            right = jnp.where(even_x, take(got_a), take(got_b))[:2]
            if q == 3:
                left, right = left * has_left, right * has_right
            strip = jnp.concatenate([left, take(own), right], axis=0)
            middle[q, y] = strip
        low, high = middle[q, 0], middle[q, cells_y - 1]
        send_c[pl.ds(q * wide, wide), :] = jnp.where(even_x, low, high)
        send_d[pl.ds(q * wide, wide), :] = jnp.where(even_x, high, low)


def half_wave(radius):
    angle = (jnp.clip(radius, 2.7, 3.0) - 2.85) * (half_pi / 0.15)
    square = angle * angle
    sine, cosine = 0.0, 0.0
    for odd in (15, 13, 11, 9, 7, 5, 3, 1):
        factor_s = 1.0
        for n in range(2, odd + 1):
            factor_s /= n
        factor_c = factor_s * odd
        sign = -1.0 if odd % 4 == 3 else 1.0
        sine = sine * square + sign * factor_s
        cosine = cosine * square + sign * factor_c
    return sine * angle, cosine


def step_gate(value):
    return jnp.where(value > 1.0, 1.0, jnp.where(value == 1.0, 0.5, 0.0))


def column_gradients(center, occupied, nearby):
    entries = len(nearby)
    each = range(entries)
    inverse, gate_r, weight, slope, unit, repulse, attract = [], [], [], [], [], [], []
    for m in each:
        offset = [nearby[m][q] - center[q] for q in range(3)]
        square = offset[0] * offset[0] + offset[1] * offset[1] + offset[2] * offset[2]
        bounded = jnp.maximum(square, 1.0)
        radius = jnp.sqrt(bounded)
        inverse.append(1.0 / radius)
        gate_r.append(step_gate(square))
        sine, cosine = half_wave(radius)
        inside, outside = radius < 2.7, radius > 3.0
        weight.append(jnp.where(inside, 1.0, jnp.where(outside, 0.0, 0.5 - 0.5 * sine)))
        slope.append(jnp.where(inside | outside, 0.0, (-0.5 * half_pi / 0.15) * cosine))
        unit.append([offset[q] * inverse[m] for q in range(3)])
        repulse.append(repulse_a * jnp.exp(-decay_one * radius))
        attract.append(attract_b * jnp.exp(-decay_two * radius))
    zero = jnp.zeros_like(occupied)
    total = [zero for _ in each]
    angular, tilt = {}, {}
    for m in each:
        for k in range(m + 1, entries):
            cosine = sum(unit[m][q] * unit[k][q] for q in range(3))
            lean = coeff_h - cosine
            spread = lean * lean
            part = 1.0 / (coeff_d2 + spread)
            value = 1.0 + (coeff_c2 / coeff_d2) * (spread * part)
            angular[m, k] = value
            tilt[m, k] = (-2.0 * coeff_c2) * lean * (part * part)
            total[m] = total[m] + weight[k] * value
            total[k] = total[k] + weight[m] * value
    half = 0.5 * occupied
    pull, by_weight, by_radius = [], [], []
    for m in each:
        bond_sum = jnp.maximum(total[m], 1.0)
        power = jnp.exp(expo_n * jnp.log(beta_t * bond_sum))
        bond = jnp.exp((-0.5 / expo_n) * jnp.log(1.0 + power))
        loss = 0.5 * bond * power / ((1.0 + power) * bond_sum)
        pull.append(half * weight[m] * attract[m] * loss * step_gate(total[m]))
        by_weight.append(half * (repulse[m] - attract[m] * bond))
        by_radius.append(
            half * weight[m] * (decay_two * attract[m] * bond - decay_one * repulse[m])
        )
    by_unit = [[zero] * 3 for _ in each]
    for m in each:
        for k in range(m + 1, entries):
            by_weight[m] = by_weight[m] + pull[k] * angular[m, k]
            by_weight[k] = by_weight[k] + pull[m] * angular[m, k]
            turn = (pull[m] * weight[k] + pull[k] * weight[m]) * tilt[m, k]
            for q in range(3):
                by_unit[m][q] = by_unit[m][q] + turn * unit[k][q]
                by_unit[k][q] = by_unit[k][q] + turn * unit[m][q]
    grads = []
    for m in each:
        across = [by_unit[m][q] * inverse[m] for q in range(3)]
        along = sum(across[q] * unit[m][q] for q in range(3))
        reach = gate_r[m] * (by_radius[m] + by_weight[m] * slope[m] - along)
        grads.append([across[q] + unit[m][q] * reach for q in range(3)])
    return grads


def near_kernel(
    middle, got_a, got_b, lists, centre, nearby, slot_at, cell_at, spots, cells, table, index, *, cells_x, cells_y
):
    entries, slots = lists.shape[0], lists.shape[3]
    shift = slots.bit_length() - 1
    even_x = lax.rem(lax.axis_index("gx"), 2) == 0
    near = cells_x + 2
    centers = near * cells_y
    base = 4 * cells_x * cells_y
    for m in range(entries):
        here = pl.ds(base + m * cells_y, cells_y)
        left = jnp.where(even_x, got_b[here, :], got_a[here, :]).astype(jnp.int32)
        right = jnp.where(even_x, got_a[here, :], got_b[here, :]).astype(jnp.int32)
        for y in range(cells_y):
            index[m, pl.ds(y * near, 1), :] = left[y : y + 1]
            for x in range(cells_x):
                index[m, pl.ds(y * near + 1 + x, 1), :] = lists[m, x, pl.ds(y, 1), :]
            index[m, pl.ds(y * near + near - 1, 1), :] = right[y : y + 1]
    for y in range(cells_y):
        strip = [middle[q, y] for q in range(4)]
        centre[3, pl.ds(y * near, near), :] = strip[3][1 : 1 + near]
        strip[2] = jnp.where(strip[3] > 0.0, strip[2], far_away)
        for q in range(3):
            for move in range(3):
                table[q, move, pl.ds((y + 1) * near, near), :] = strip[q][move : move + near]
    for q in range(3):
        for move in range(3):
            for y in (0, cells_y + 1):
                table[q, move, pl.ds(y * near, near), :] = jnp.zeros((near, slots), jnp.float32)
        centre[q] = table[q, 1, pl.ds(near, centers), :]
    line = lax.broadcasted_iota(jnp.int32, (centers, slots), 0)
    for m in range(entries):
        value = index[m]
        slot, cell = value & (slots - 1), value >> shift
        picked = []
        for c in range(9):
            for q in range(3):
                source = table[q, c // 3, pl.ds((c % 3) * near, centers), :]
                got = jnp.take_along_axis(source, slot, axis=1, mode="promise_in_bounds")
                if c == 0:
                    picked.append(got)
                else:
                    picked[q] = jnp.where(cell == c, got, picked[q])
        for q in range(3):
            nearby[m, q] = picked[q]
        move_x = jnp.where(cell < 3, 0, jnp.where(cell < 6, 1, 2))
        move_y = cell - 3 * move_x
        away = ((line < near) & (move_y == 0)) | ((line >= centers - near) & (move_y == 2))
        slot_at[m] = slot
        cell_at[m] = jnp.where(away, move_x, 3)
        spots[pl.ds(m * centers, centers), :] = slot.astype(jnp.float32)
        cells[pl.ds(m * centers, centers), :] = cell.astype(jnp.float32)


def force_kernel(
    rows, centre, nearby_own, slot_at, cell_at, spots, cells, got_c, got_d, *refs,
    counts, cells_x, cells_y, capacity, turns
):
    outs = refs[: len(turns) + 1] if turns else refs[:1]
    table, parts = refs[len(outs) :]
    entries, centers, slots = slot_at.shape
    at_y = lax.axis_index("gy")
    even_x = lax.rem(lax.axis_index("gx"), 2) == 0
    wide, near = cells_x + 4, cells_x + 2
    has_below, has_above = at_y > 0, at_y < counts[1] - 1
    for row, swap, there in (
        (0, even_x, has_below),
        (centers - near, jnp.logical_not(even_x), has_above),
    ):
        strip = [
            jnp.where(swap, got_d[pl.ds(q * wide, wide), :], got_c[pl.ds(q * wide, wide), :])
            for q in range(4)
        ]
        full = strip[3] * there.astype(jnp.float32) > 0.0
        strip[2] = jnp.where(full, strip[2], far_away)
        for move in range(3):
            for q in range(3):
                table[q, move, pl.ds(row, near), :] = strip[q][move : move + near]
    for y in range(1, cells_y - 1):
        for move in range(3):
            for q in range(3):
                table[q, move, pl.ds(y * near, near), :] = jnp.zeros((near, slots), jnp.float32)
    center = [centre[q] for q in range(3)]
    occupied = centre[3]
    nearby = []
    for m in range(entries):
        picked = [nearby_own[m, q] for q in range(3)]
        slot, cell = slot_at[m], cell_at[m]
        for move in range(3):
            for q in range(3):
                got = jnp.take_along_axis(table[q, move], slot, axis=1, mode="promise_in_bounds")
                picked[q] = jnp.where(cell == move, got, picked[q])
        nearby.append(picked)
    grads = column_gradients(center, occupied, nearby)
    own = [sum(grads[m][q] for m in range(entries)) for q in range(3)]
    zero = jnp.zeros_like(occupied)

    def part(m, row):
        return pl.ds((m * ROWS + row) * centers, centers)

    def column_parts(m, i):
        return parts[pl.ds(m * ROWS * centers + i, ROWS, stride=centers), :]

    for m in range(entries):
        for q in range(3):
            high = grads[m][q].astype(jnp.bfloat16).astype(jnp.float32)
            parts[part(m, 3 + q), :] = high
            parts[part(m, q), :] = grads[m][q] - high
        for row in (6, 7):
            parts[part(m, row), :] = zero
    for q in range(3):
        parts[part(entries, 3 + q), :] = own[q]
    for row in (0, 1, 2, 6, 7):
        parts[part(entries, row), :] = zero
    step = 16
    ramps = [
        (lax.broadcasted_iota(jnp.int32, (step, slots), 0) + first).astype(jnp.float32).astype(jnp.bfloat16)
        for first in range(0, slots, step)
    ]
    one, none = jnp.ones((step, slots), jnp.bfloat16), jnp.zeros((step, slots), jnp.bfloat16)
    targets = [(x, y) for x in range(cells_x) for y in range(-1, cells_y + 1)]
    empty = jnp.zeros((ROWS, slots), jnp.float32)
    hot, values_at = [], []
    for y in range(cells_y):
        for x in range(-1, cells_x + 1):
            i = y * near + x + 1
            for m in range(entries):
                row = spots[pl.ds(m * centers + i, step, stride=0), :].astype(jnp.bfloat16)
                hot.append(
                    jnp.concatenate([jnp.where(ramp == row, one, none) for ramp in ramps], axis=0)
                )
                values = column_parts(m, i)
                cell = cells[pl.ds(m * centers + i, ROWS, stride=0), :]
                masked = []
                for to_x, to_y in targets:
                    dx, dy = to_x - x, to_y - y
                    near_by = -1 <= dx <= 1 and -1 <= dy <= 1
                    c = float((dx + 1) * 3 + dy + 1)
                    masked.append(jnp.where(cell == c, values, 0.0) if near_by else empty)
                values_at.append(jnp.concatenate(masked, axis=0).astype(jnp.bfloat16))
    sums = jnp.transpose(lax.dot_general(
        jnp.concatenate(hot, axis=1),
        jnp.concatenate(values_at, axis=1),
        (((1,), (1,)), ((), ())),
        preferred_element_type=jnp.float32,
    ))
    reached = {key: sums[n * ROWS : (n + 1) * ROWS] for n, key in enumerate(targets)}
    line = lax.broadcasted_iota(jnp.int32, (ROWS, slots), 0)
    kick = half_step * force_scale
    chosen = (line >= 3) & (line < 6)
    columns, ghosts = [], []
    for x in range(cells_x):
        for y in range(-1, cells_y + 1):
            block = reached[x, y]
            block = block + pltpu.roll(block, 3, 0)
            if 0 <= y < cells_y:
                block = column_parts(entries, y * near + x + 1) - block
                column = rows[pl.ds((x * cells_y + y) * ROWS, ROWS), :]
                column = column + jnp.where(chosen, kick * block, 0.0)
                named = jnp.broadcast_to(column[7:], (ROWS, slots))
                columns.append((named, jnp.where(line == 7, float(x * cells_y + y + 1), column)))
            else:
                ghosts.append((-kick * block)[3:6])

    def message(owner):
        pieces = []
        for slot in range(capacity):
            wanted = (owner * capacity + slot).astype(jnp.float32)
            pieces.append(sum(jnp.where(named == wanted, column, 0.0) for named, column in columns))
        return pieces + ghosts

    def write(ref, pieces):
        first = 0
        for piece in pieces:
            ref[pl.ds(first, piece.shape[0]), :] = piece
            first += piece.shape[0]

    if turns:
        for ref, turn in zip(outs[:-1], turns):
            write(ref, message(named_by(turn, at_y)))
        write(outs[-1], message(at_y))
    else:
        for owner in range(counts[1]):
            write(outs[0].at[owner], message(jnp.int32(owner)))


def gather_kernel(*refs, count, cells_x, cells_y, capacity, turns):
    at_y = lax.axis_index("gy")
    if turns:
        ins, out, held = refs[:-2], refs[-2], refs[-1]
        for ref, turn in zip(ins[:-1], turns):
            held[named_by([turn.index(n) for n in range(count)], at_y)] = ref[...]
        held[at_y] = ins[-1][...]
    else:
        held, out = refs
    first = capacity * ROWS
    for source in range(count):
        for slot in range(capacity):
            block = held[source, pl.ds(slot * ROWS, ROWS), :]
            name = held[source, pl.ds(slot * ROWS + 7, 3, stride=0), :]
            speed = block[3:6]
            for x in range(cells_x):
                for other, y, side in ((source + 1, cells_y - 1, 0), (source - 1, 0, 1)):
                    if 0 <= other < count:
                        part = held[other, pl.ds(first + (2 * x + side) * 3, 3), :]
                        speed = speed + jnp.where(name == float(x * cells_y + y + 1), part, 0.0)
            lines = pl.ds(source * 7 * capacity + slot, 7, stride=capacity)
            out[lines, :] = jnp.concatenate([block[:3], speed, block[6:7]], axis=0)


def per_device(displacement, velocity, forces, heights, counts, neighbours, plan):
    cells_x, cells_y, slots = heights.shape
    entries = neighbours.shape[0]
    sizes = (lax.axis_size("gx"), lax.axis_size("gy"))
    columns = cells_x * cells_y
    capacity = max(2, (2 * columns + sizes[1] - 1) // sizes[1])
    inputs = (displacement, velocity, forces, heights, counts, neighbours, plan.reshape(1, columns))
    whole = pl.BlockSpec(memory_space=VMEM)
    shape = lambda *dims: jax.ShapeDtypeStruct(dims, jnp.float32)
    wide, near = cells_x + 4, cells_x + 2
    centers = near * cells_y

    def swap(value, pairs):
        return lax.ppermute(value, ("gx", "gy"), pairs)

    first_size = 4 * columns + entries * cells_y
    rows, send_a, send_b = pl.pallas_call(
        functools.partial(prepare_kernel, capacity=capacity),
        out_shape=(shape(columns * ROWS, slots), shape(first_size, slots), shape(first_size, slots)),
        in_specs=[pl.BlockSpec(memory_space=HBM)] * len(inputs),
        out_specs=(whole, whole, whole),
        scratch_shapes=[
            pltpu.VMEM((3,) + displacement.shape, jnp.float32),
            pltpu.VMEM((entries + 1,) + heights.shape, jnp.int32),
            pltpu.SMEM(counts.shape, jnp.int32),
            pltpu.SMEM((1, columns), jnp.int32),
            pltpu.SemaphoreType.DMA((4,)),
        ],
        compiler_params=pltpu.CompilerParams(vmem_limit_bytes=VMEM_BYTES),
        name="prepare",
    )(*[pltpu.with_memory_space_constraint(value, HBM) for value in inputs])
    got_a = swap(send_a, exchange_pairs(sizes, 0, False))
    got_b = swap(send_b, exchange_pairs(sizes, 0, True))
    second_size = 4 * wide
    middle, send_c, send_d = pl.pallas_call(
        functools.partial(strip_kernel, count_x=sizes[0], cells_x=cells_x, cells_y=cells_y),
        out_shape=(shape(4, cells_y, wide, slots), shape(second_size, slots), shape(second_size, slots)),
        in_specs=[whole] * 3,
        out_specs=(whole, whole, whole),
        compiler_params=pltpu.CompilerParams(vmem_limit_bytes=VMEM_BYTES),
        name="strips",
    )(send_a, got_a, got_b)
    got_c = swap(send_c, circle_pairs(sizes, 1))
    got_d = swap(send_d, circle_pairs(sizes, 0))
    turns = rounds(sizes[1])
    size = capacity * ROWS + 6 * cells_x
    out_shape = (shape(size, slots),) * (len(turns) + 1) if turns else (shape(sizes[1], size, slots),)
    flat = lambda kind, *dims: jax.ShapeDtypeStruct(dims, kind)
    found = pl.pallas_call(
        functools.partial(near_kernel, cells_x=cells_x, cells_y=cells_y),
        out_shape=(
            shape(4, centers, slots),
            shape(entries, 3, centers, slots),
            flat(jnp.int32, entries, centers, slots),
            flat(jnp.int32, entries, centers, slots),
            shape(entries * centers, slots),
            shape(entries * centers, slots),
        ),
        in_specs=[whole] * 4,
        out_specs=(whole,) * 6,
        scratch_shapes=[
            pltpu.VMEM((3, 3, near * (cells_y + 2), slots), jnp.float32),
            pltpu.VMEM((entries, centers, slots), jnp.int32),
        ],
        compiler_params=pltpu.CompilerParams(vmem_limit_bytes=VMEM_BYTES),
        cost_estimate=pl.CostEstimate(flops=1000000, bytes_accessed=200000, transcendentals=0),
        name="near",
    )(middle, got_a, got_b, neighbours)
    sent = pl.pallas_call(
        functools.partial(
            force_kernel, counts=sizes, cells_x=cells_x, cells_y=cells_y, capacity=capacity, turns=turns
        ),
        out_shape=out_shape,
        in_specs=[whole] * 9,
        out_specs=tuple(whole for _ in out_shape),
        scratch_shapes=[
            pltpu.VMEM((3, 3, centers, slots), jnp.float32),
            pltpu.VMEM(((entries + 1) * ROWS * centers, slots), jnp.float32),
        ],
        compiler_params=pltpu.CompilerParams(vmem_limit_bytes=VMEM_BYTES),
        name="forces",
    )(rows, *found, got_c, got_d)
    if turns:
        arrived = [lax.ppermute(value, "gy", list(enumerate(turn))) for value, turn in zip(sent, turns)]
        arrived.append(sent[-1])
        scratch = [pltpu.VMEM((sizes[1], size, slots), jnp.float32)]
    else:
        arrived = [lax.all_to_all(sent[0], "gy", split_axis=0, concat_axis=0, tiled=True)]
        scratch = []
    result = pl.pallas_call(
        functools.partial(
            gather_kernel, count=sizes[1], cells_x=cells_x, cells_y=cells_y, capacity=capacity, turns=turns
        ),
        out_shape=shape(sizes[1] * 7 * capacity, slots),
        in_specs=[whole] * len(arrived),
        out_specs=whole,
        scratch_shapes=scratch,
        compiler_params=pltpu.CompilerParams(vmem_limit_bytes=VMEM_BYTES),
        name="collect",
    )(*arrived)
    return jnp.swapaxes(result.reshape(sizes[1], 7, capacity, slots), 1, 2)[None, None]


def solution(mesh):
    in_specs = (
        P(None, "gx", "gy", None),
        P(None, "gx", "gy", None),
        P(None, "gx", "gy", None),
        P("gx", "gy", None),
        P("gx", "gy"),
        P(None, "gx", "gy", None),
        P("gx", "gy", None, None),
    )
    out_specs = P("gx", "gy", None, None, None, None)
    return jax.shard_map(
        per_device, mesh=mesh, in_specs=in_specs, out_specs=out_specs, check_vma=False
    )
```
